256 devices in a mesh: grp: 8 (over x, core), dev: 32 (over y, z).
Axes of the slice: x: 4, y: 4, z: 8, core: 2. Of those that a mesh axis runs over, the one named last changes fastest.
Arguments:
- queries: bfloat16 [65536, 768], P(('grp', 'dev')), may hold values from -1.796875 to 1.796875
- query_slots: int32 [65536], P('grp'), may hold values from 0 to 8191, as said below
- w_res: bfloat16 [768, 768], replicated, may hold values from -0.21875 to 0.21875
- labels: bfloat16 [5120, 128, 768], P(('grp', 'dev')), may hold values from -0.71875 to 0.71875
- blocks: int32 [512, 12], P('grp'), may hold values from 0 to 5119, as said below
- positives: int32 [65536, 4], P(('grp', 'dev')), may hold values from 0 to 655359, as said below
Outputs:
- query_loss: float32 [65536], P(('grp', 'dev'))
- query_grad: bfloat16 [65536, 768], P(('grp', 'dev'))
- label_grad: bfloat16 [5120, 128, 768], P(('grp', 'dev'))
- residual_grad: bfloat16 [768, 768], replicated
The draws below stay inside these ranges and needn't reach their ends.
Inputs may be any that keep to these rules, and one draw needn't show every extreme that they name: `query_slots`: the rows of one grp index (rows g * 256 * 32 onward) hold a permutation of 0 to 8191; a place // 256 is the dev index that owns the query's cluster, and the 256 rows of every device send exactly 8 queries to each owner. Row c lists 12 different blocks, all held by devices of the same grp index as the cluster's owner (device c // 2). The 2 clusters of one device list at most 16 distinct blocks, of which at most 1 are held by any one device; for every device's clusters some holder reaches 1. `positives`: the 4 labels of row r are different and lie in 4 different blocks listed for cluster r // 128.
All inputs are finite; a program needn't handle non-finite values.
Results may differ from the reference program's by a relative error of at most 0.0047.
The reference program's roundings to bfloat16 on the way (of `hidden`, `clustered`, `errors`, `cluster_grad`, `partial`, `hidden_grad` and `pre_grad`) count: a program that leaves them out, or rounds other values in their place, can miss the bound.
Values may be sent and summed in bfloat16 or wider, within the bound.
No kernel may reach another device: no remote copies, remote signals or barrier semaphores. Data moves between devices by JAX's collectives and lax.ppermute only.
A program may use at most 128 MiB of HBM per device.

```python
from functools import partial
import jax
import jax.numpy as jnp
from jax import lax

D = 768
BLK = 128
CSIZE = 128
SHORT = 12
NPOS = 4
POOL = 16
BLK_DEV = 20
CL_DEV = 2
Q_DEV = 256
CAPU = 1
QUERIES = 65536
CLUSTERS = 512
NBLK = 5120
N_GRP = 8
N_DEV = 32
DEVICES = 256


def pool_lists(key):

    def one_device(device_key, device):
        owner_key, base_key, pick_key = jax.random.split(device_key, 3)
        spread = jnp.repeat(jnp.arange(N_DEV, dtype=jnp.int32), CAPU)
        owners = jax.random.permutation(owner_key, spread)[:POOL]
        positions = jnp.arange(POOL, dtype=jnp.int32)
        earlier = positions[None, :] < positions[:, None]
        ranking = jnp.sum((owners[:, None] == owners[None, :]) & earlier, axis=1).astype(jnp.int32)
        starts = jax.random.randint(base_key, (N_DEV,), 0, BLK_DEV, dtype=jnp.int32)
        within = (starts[owners] + ranking) % BLK_DEV
        group_number = device // N_DEV
        pool_ids = (group_number * N_DEV + owners) * BLK_DEV + within
        counts = jnp.sum(owners[:, None] == jnp.arange(N_DEV, dtype=jnp.int32)[None, :], axis=0)
        busiest = jnp.argmax(counts).astype(jnp.int32)
        forced = (owners == busiest).astype(jnp.int32)

        def one_cluster(cluster_key):
            score_key, order_key = jax.random.split(cluster_key)
            scores = jax.random.permutation(score_key, POOL).astype(jnp.int32) - POOL * forced
            picked = jnp.argsort(scores)[:SHORT]
            return jax.random.permutation(order_key, pool_ids[picked])
        return jax.vmap(one_cluster)(jax.random.split(pick_key, CL_DEV))
    devices_all = jnp.arange(DEVICES, dtype=jnp.int32)
    device_keys = jax.vmap(partial(jax.random.fold_in, key))(devices_all)
    return jax.vmap(one_device)(device_keys, devices_all).reshape(CLUSTERS, SHORT).astype(jnp.int32)


def draw_blocks(key, part):
    return pool_lists(jax.random.fold_in(key, 7))


def draw_positives(key, part):
    lists = pool_lists(jax.random.fold_in(key, 7))
    start_key, label_key = jax.random.split(jax.random.fold_in(key, 11))
    cluster_of = jnp.arange(QUERIES, dtype=jnp.int32) // CSIZE
    starts = jax.random.randint(start_key, (QUERIES,), 0, SHORT, dtype=jnp.int32)
    columns = (starts[:, None] + jnp.arange(NPOS, dtype=jnp.int32)[None, :]) % SHORT
    inside = jax.random.randint(label_key, (QUERIES, NPOS), 0, BLK, dtype=jnp.int32)
    return (lists[cluster_of[:, None], columns] * BLK + inside).astype(jnp.int32)


def draw_query_slots(key, part):
    per_peer = Q_DEV // N_DEV
    group_rows = Q_DEV * N_DEV

    def one_group(group_key):
        dest_key, place_key = jax.random.split(group_key)
        base_row = jnp.repeat(jnp.arange(N_DEV, dtype=jnp.int32), per_peer)
        dest_keys = jax.random.split(dest_key, N_DEV)
        targets = jax.vmap(jax.random.permutation, (0, None))(dest_keys, base_row).reshape(group_rows)
        sort_keys = targets * group_rows + jnp.arange(group_rows, dtype=jnp.int32)
        order = jnp.argsort(sort_keys)
        place_keys = jax.random.split(place_key, N_DEV)
        shuffles = jax.vmap(jax.random.permutation, (0, None))(place_keys, jnp.arange(Q_DEV, dtype=jnp.int32))
        sorted_owner = jnp.arange(group_rows, dtype=jnp.int32) // Q_DEV
        sorted_slots = sorted_owner * Q_DEV + shuffles.reshape(group_rows)
        return jnp.zeros((group_rows,), jnp.int32).at[order].set(sorted_slots.astype(jnp.int32))
    group_keys = jax.random.split(key, DEVICES // N_DEV)
    return jax.vmap(one_group)(group_keys).reshape(QUERIES).astype(jnp.int32)


def shard_levels(rng, dims, shards, smallest, high):
    loudness, own = 1.0, jax.random.fold_in(rng, 6)
    for axis_at, shards_of in shards:
        heights = jnp.exp(jax.random.uniform(jax.random.fold_in(own, axis_at), (shards_of,), jnp.float32, smallest / len(shards), high / len(shards)))
        loudness = loudness * jnp.repeat(heights, dims[axis_at] // shards_of).reshape([-1 if axis == axis_at else 1 for axis in range(len(dims))])
    return loudness


def scatter_about(stream_key, extent, deviation, most, cuts=(), kind=jnp.bfloat16):
    values = jax.random.normal(stream_key, extent, jnp.float32) * deviation
    if len(cuts) > 0:
        values = shard_levels(stream_key, extent, cuts, -0.22, 0.18) * values
    return jnp.clip(values, min=-most, max=most).astype(kind)


def setup_inputs(seed: int = 0) -> dict:
    streams_of = jax.random.split(jax.random.key(seed), 7)
    return {
        "queries": scatter_about(streams_of[0], (QUERIES, D), 0.3, 1.796875, ((0, 256),)),
        "query_slots": draw_query_slots(jax.random.fold_in(streams_of[6], 71), 0),
        "w_res": scatter_about(streams_of[2], (D, D), D ** -0.5, 0.21875),
        "labels": scatter_about(streams_of[3], (NBLK, BLK, D), 0.12, 0.71875, ((0, 256),)),
        "blocks": draw_blocks(jax.random.fold_in(streams_of[6], 71), 0),
        "positives": draw_positives(jax.random.fold_in(streams_of[6], 71), 0),
    }


def activate(values):
    return jax.nn.gelu(values, approximate=True)

def activate_slope(values):
    return jax.vjp(activate, values)[1](jnp.ones_like(values))[0]

def reference(queries, query_slots, w_res, labels, blocks, positives):
    group_rows = Q_DEV * N_DEV
    group_clusters = CL_DEV * N_DEV
    group_blocks = BLK_DEV * N_DEV
    offsets = jnp.arange(BLK, dtype=jnp.int32)

    def group_step(weight_total, inputs):
        group_number, group_input, places, lists, wanted, group_labels = inputs
        pre = jnp.dot(group_input, w_res, preferred_element_type=jnp.float32)
        hidden = (group_input.astype(jnp.float32) + activate(pre)).astype(jnp.bfloat16)
        clustered = jnp.zeros_like(hidden).at[places].set(hidden)
        block_base = group_number * group_blocks

        def device_step(totals, pieces):
            cluster_rows, cluster_ids, cluster_pos = pieces
            local_ids = (cluster_ids - block_base).astype(jnp.int32)
            chosen = group_labels[local_ids]
            rows_wide = cluster_rows.astype(jnp.float32)
            chosen_wide = chosen.astype(jnp.float32)
            logits = jnp.einsum('cqd,ckjd->cqkj', rows_wide, chosen_wide, precision=lax.Precision.HIGHEST)
            label_ids = cluster_ids[:, :, None] * BLK + offsets[None, None, :]
            hits = label_ids[:, None, :, :, None] == cluster_pos[:, :, None, None, :]
            targets = jnp.any(hits, axis=-1).astype(jnp.float32)
            loss_rows = lax.optimization_barrier(jnp.mean(jax.nn.softplus(logits) - targets * logits, axis=(2, 3)))
            errors = (jax.nn.sigmoid(logits) - targets).astype(jnp.bfloat16)
            errors_wide = errors.astype(jnp.float32)
            grad_rows = jnp.einsum('cqkj,ckjd->cqd', errors_wide, chosen_wide, precision=lax.Precision.HIGHEST).astype(jnp.bfloat16)
            terms = jnp.einsum('cqkj,cqd->ckjd', errors_wide, rows_wide, precision=lax.Precision.HIGHEST)
            terms = terms.reshape(-1, BLK, D)
            flat_ids = local_ids.reshape(-1)
            same_block = flat_ids[:, None] == flat_ids[None, :]
            first_seen = jnp.argmax(same_block, axis=1).astype(jnp.int32)
            summed = jax.ops.segment_sum(terms, first_seen, num_segments=flat_ids.shape[0])
            rounded = lax.optimization_barrier(summed.astype(jnp.bfloat16)).astype(jnp.float32)
            totals = totals.at[flat_ids].add(rounded)
            return (totals, (loss_rows, grad_rows))
        start = jnp.zeros((group_blocks, BLK, D), jnp.float32)
        pieces = (clustered.reshape(N_DEV, CL_DEV, CSIZE, D), lists.reshape(N_DEV, CL_DEV, SHORT), wanted.reshape(N_DEV, CL_DEV, CSIZE, NPOS))
        totals, (loss_rows, grad_rows) = lax.scan(device_step, start, pieces)
        cluster_grad = grad_rows.reshape(group_rows, D)
        hidden_grad = cluster_grad[places]
        pre_grad = (hidden_grad.astype(jnp.float32) * activate_slope(pre)).astype(jnp.bfloat16)
        back_term = jnp.dot(pre_grad, w_res.T, preferred_element_type=jnp.float32)
        query_grad = (hidden_grad.astype(jnp.float32) + back_term).astype(jnp.bfloat16)
        weight_total = weight_total + jnp.dot(group_input.T, pre_grad, preferred_element_type=jnp.float32)
        return (weight_total, (loss_rows.reshape(group_rows), query_grad, totals.astype(jnp.bfloat16)))
    inputs = (jnp.arange(N_GRP, dtype=jnp.int32), queries.reshape(N_GRP, group_rows, D), query_slots.reshape(N_GRP, group_rows), blocks.reshape(N_GRP, group_clusters, SHORT), positives.reshape(N_GRP, group_rows, NPOS), labels.reshape(N_GRP, group_blocks, BLK, D))
    weight_total, (loss_rows, query_grad, label_grad) = lax.scan(group_step, jnp.zeros((D, D), jnp.float32), inputs)
    residual_grad = (weight_total * QUERIES ** (-0.5)).astype(jnp.bfloat16)
    return (loss_rows.reshape(QUERIES), query_grad.reshape(QUERIES, D), label_grad.reshape(NBLK, BLK, D), residual_grad)
```

```python
import jax
import jax.numpy as jnp
import numpy as np
from jax import lax
from jax.experimental import pallas as pl
from jax.experimental.pallas import tpu as pltpu
from jax.sharding import Mesh, PartitionSpec as P

D = 768
HALF = D // 2
BLK = 128
CSIZE = 128
SHORT = 12
NPOS = 4
BLK_DEV = 20
ENC = 128
NY = 4
NZ = 8
NDEV = NY * NZ
ROWS = 2 * CSIZE
PER = ROWS // NDEV
GRP_BLOCKS = NDEV * BLK_DEV

F32 = jnp.float32
BF16 = jnp.bfloat16


def activate(values):
    return jax.nn.gelu(values, approximate=True)


def activate_slope(values):
    return jax.vjp(activate, values)[1](jnp.ones_like(values))[0]


def wanted_of(wanted_ref, y, delta, zo):
    owner = lax.rem(y + delta, NY) * NZ + zo
    return jnp.maximum(wanted_ref[2 * owner], wanted_ref[2 * owner + 1])


def pack_kernel(wanted_ref, place_ref, labels, down, up, far_a, far_b, held, in_sem, out_sem):
    y = place_ref[0]
    ins = []
    for slot in range(3 * NZ):
        delta = (NY - 1, 1, 2)[slot // NZ]
        pick = jnp.maximum(wanted_of(wanted_ref, y, delta, slot % NZ), 0)
        copy = pltpu.make_async_copy(labels.at[pick], held.at[slot], in_sem.at[slot])
        copy.start()
        ins.append(copy)
    order = list(range(2 * NZ, 3 * NZ)) + list(range(2 * NZ))
    outs = []
    for slot in order:
        ins[slot].wait()
        zo = slot % NZ
        if slot < 2 * NZ:
            target = (down, up)[slot // NZ]
            moves = [pltpu.make_async_copy(held.at[slot], target.at[zo], out_sem.at[slot])]
        else:
            moves = [
                pltpu.make_async_copy(
                    held.at[slot, :, pl.ds(0, HALF)], far_a.at[zo], out_sem.at[slot]
                ),
                pltpu.make_async_copy(
                    held.at[slot, :, pl.ds(HALF, HALF)], far_b.at[zo], out_sem.at[slot + NZ]
                ),
            ]
        for move in moves:
            move.start()
        outs.extend(moves)
    for move in outs:
        move.wait()


def pack(wanted, place, labels):
    any_spec = pl.BlockSpec(memory_space=pl.ANY)
    full = jax.ShapeDtypeStruct((NZ, BLK, D), BF16)
    half = jax.ShapeDtypeStruct((NZ, BLK, HALF), BF16)
    return pl.pallas_call(
        pack_kernel,
        out_shape=(full, full, half, half),
        grid_spec=pltpu.PrefetchScalarGridSpec(
            num_scalar_prefetch=2,
            grid=(1,),
            in_specs=[any_spec],
            out_specs=[any_spec] * 4,
            scratch_shapes=[
                pltpu.VMEM((3 * NZ, BLK, D), BF16),
                pltpu.SemaphoreType.DMA((3 * NZ,)),
                pltpu.SemaphoreType.DMA((4 * NZ,)),
            ],
        ),
        cost_estimate=pl.CostEstimate(flops=0, bytes_accessed=10_000_000, transcendentals=0),
        name="pack",
    )(wanted, place, labels)


def meet_kernel(
    table_ref, wanted_ref, place_ref,
    rows_ref, own_ref, next_ref, far_a_ref, far_b_ref, prev_ref,
    grad_ref, part0_ref, part1_ref, part2a_ref, part2b_ref, part3_ref, loss_ref,
    labs,
):
    y = place_ref[0]
    z = place_ref[1]
    zo = lax.rem(z + pl.program_id(0), NZ)
    rows = rows_ref[:, :D]
    coded = rows_ref[:, D:].astype(F32)
    ids = [
        coded[:, 3 * n : 3 * n + 1] * 16384.0
        + coded[:, 3 * n + 1 : 3 * n + 2] * 128.0
        + coded[:, 3 * n + 2 : 3 * n + 3]
        for n in range(NPOS)
    ]
    labs[0:BLK, :] = own_ref[0]
    labs[BLK : 2 * BLK, :] = next_ref[0]
    labs[2 * BLK : 3 * BLK, :HALF] = far_a_ref[0]
    labs[2 * BLK : 3 * BLK, HALF:] = far_b_ref[0]
    labs[3 * BLK : 4 * BLK, :] = prev_ref[0]
    blocks_here = labs[...]
    logits = lax.dot_general(
        rows, blocks_here, (((1,), (1,)), ((), ())), preferred_element_type=F32
    )
    row_at = lax.broadcasted_iota(jnp.int32, (ROWS, BLK), 0)
    lane_at = lax.broadcasted_iota(jnp.int32, (ROWS, BLK), 1).astype(F32)
    loss = jnp.zeros((ROWS, BLK), F32)
    errors = []
    for delta in range(NY):
        holder_y = lax.rem(y + delta, NY)
        base = (y * NZ + zo) * 2 * NY + holder_y
        first = table_ref[base]
        second = table_ref[base + NY]
        block = (jnp.maximum(first, second) * BLK).astype(F32)
        live = jnp.where(row_at < CSIZE, first, second) >= 0
        here = logits[:, delta * BLK : (delta + 1) * BLK]
        hit = jnp.zeros((ROWS, BLK), jnp.bool_)
        for n in range(NPOS):
            hit = jnp.logical_or(hit, (ids[n] - block) == lane_at)
        targets = hit.astype(F32)
        tail = jnp.exp(-jnp.abs(here))
        soft = jnp.maximum(here, 0.0) + jnp.log1p(tail)
        sig = jnp.where(here >= 0, 1.0, tail) / (1.0 + tail)
        loss += jnp.where(live, soft - targets * here, 0.0)
        errors.append(jnp.where(live, sig - targets, 0.0).astype(BF16))
    errors = jnp.concatenate(errors, axis=1)
    grad_ref[0] = jnp.dot(errors, blocks_here, preferred_element_type=F32)
    parts = lax.dot_general(
        errors, rows, (((0,), (0,)), ((), ())), preferred_element_type=F32
    ).astype(BF16)
    part0_ref[0] = parts[0:BLK]
    part1_ref[0] = parts[BLK : 2 * BLK]
    part2a_ref[0] = parts[2 * BLK : 3 * BLK, :HALF]
    part2b_ref[0] = parts[2 * BLK : 3 * BLK, HALF:]
    part3_ref[0] = parts[3 * BLK : 4 * BLK]
    sums = lax.dot_general(
        jnp.ones((8, BLK), F32), loss, (((1,), (1,)), ((), ())),
        precision=lax.Precision.HIGHEST, preferred_element_type=F32,
    )
    loss_ref[pl.ds(zo, 1), :] = sums[0:1]


def meet(table, wanted, place, gathered, labels, nxt, far_a, far_b, prev):
    def owner_of(i, place_ref):
        return lax.rem(place_ref[1] + i, NZ)

    def own_map(i, table_ref, wanted_ref, place_ref):
        pick = wanted_of(wanted_ref, place_ref[0], 0, owner_of(i, place_ref))
        return (jnp.maximum(pick, 0), 0, 0)

    def owner_map(i, table_ref, wanted_ref, place_ref):
        return (owner_of(i, place_ref), 0, 0)

    full = pl.BlockSpec((1, BLK, D), owner_map)
    half = pl.BlockSpec((1, BLK, HALF), owner_map)
    full_shape = jax.ShapeDtypeStruct((NZ, BLK, D), BF16)
    half_shape = jax.ShapeDtypeStruct((NZ, BLK, HALF), BF16)
    return pl.pallas_call(
        meet_kernel,
        out_shape=(
            jax.ShapeDtypeStruct((NZ, ROWS, D), F32),
            full_shape, full_shape, half_shape, half_shape, full_shape,
            jax.ShapeDtypeStruct((NZ, ROWS), F32),
        ),
        grid_spec=pltpu.PrefetchScalarGridSpec(
            num_scalar_prefetch=3,
            grid=(NZ,),
            in_specs=[
                pl.BlockSpec((ROWS, D + ENC), lambda i, t, w, p: (owner_of(i, p), 0)),
                pl.BlockSpec((1, BLK, D), own_map),
                full, half, half, full,
            ],
            out_specs=[
                pl.BlockSpec((1, ROWS, D), lambda i, t, w, p: (i, 0, 0)),
                full, full, half, half, full,
                pl.BlockSpec((NZ, ROWS), lambda i, t, w, p: (0, 0)),
            ],
            scratch_shapes=[pltpu.VMEM((NY * BLK, D), BF16)],
        ),
        cost_estimate=pl.CostEstimate(
            flops=5_000_000_000, bytes_accessed=25_000_000, transcendentals=3_000_000
        ),
        name="meet",
    )(table, wanted, place, gathered, labels, nxt, far_a, far_b, prev)


def fold_kernel(wanted_ref, place_ref, own, up, far_a, far_b, down, out, total):
    y = place_ref[0]
    total[...] = jnp.zeros_like(total)

    def one(zo, carry):
        for delta in range(NY):
            pick = wanted_of(wanted_ref, y, delta, zo)

            @pl.when(pick >= 0)
            def _():
                if delta == 2:
                    total[pick, :, :HALF] += far_a[zo].astype(F32)
                    total[pick, :, HALF:] += far_b[zo].astype(F32)
                else:
                    total[pick] += (own, up, None, down)[delta][zo].astype(F32)

        return carry

    lax.fori_loop(0, NZ, one, 0)

    def put(b, carry):
        out[b] = total[b].astype(BF16)
        return carry

    lax.fori_loop(0, BLK_DEV, put, 0)


def fold(wanted, place, own, up, far_a, far_b, down):
    vmem = pl.BlockSpec(memory_space=pltpu.VMEM)
    return pl.pallas_call(
        fold_kernel,
        out_shape=jax.ShapeDtypeStruct((BLK_DEV, BLK, D), BF16),
        grid_spec=pltpu.PrefetchScalarGridSpec(
            num_scalar_prefetch=2,
            grid=(1,),
            in_specs=[
                pl.BlockSpec((NZ, BLK, D), lambda i, w, p: (0, 0, 0)),
                pl.BlockSpec((NZ, BLK, D), lambda i, w, p: (0, 0, 0)),
                pl.BlockSpec((NZ, BLK, HALF), lambda i, w, p: (0, 0, 0)),
                pl.BlockSpec((NZ, BLK, HALF), lambda i, w, p: (0, 0, 0)),
                pl.BlockSpec((NZ, BLK, D), lambda i, w, p: (0, 0, 0)),
            ],
            out_specs=pl.BlockSpec((BLK_DEV, BLK, D), lambda i, w, p: (0, 0, 0)),
            scratch_shapes=[pltpu.VMEM((BLK_DEV, BLK, D), F32)],
        ),
        cost_estimate=pl.CostEstimate(flops=5_000_000, bytes_accessed=25_000_000, transcendentals=0),
        compiler_params=pltpu.CompilerParams(vmem_limit_bytes=48 * 1024 * 1024),
        name="fold",
    )(wanted, place, own, up, far_a, far_b, down)


def shift(values, axis, amount):
    size = lax.axis_size(axis)
    return lax.ppermute(values, axis, [(i, (i + amount) % size) for i in range(size)])


def scatter_sum(values, axis):
    size = lax.axis_size(axis)
    me = lax.axis_index(axis)
    step = values.shape[0] // size

    def piece(amount):
        at = lax.rem(me + amount, size) * step
        return lax.dynamic_slice_in_dim(values, at, step, 0)

    total = piece(0)
    for got in [shift(piece(amount), axis, amount) for amount in range(1, size)]:
        total = total + got
    return total


def gather_rows(values, axis):
    size = lax.axis_size(axis)
    me = lax.axis_index(axis)
    step = values.shape[0]
    out = jnp.zeros((size * step,) + values.shape[1:], values.dtype)
    out = lax.dynamic_update_slice_in_dim(out, values, me * step, 0)
    for amount in range(1, size):
        got = shift(values, axis, amount)
        out = lax.dynamic_update_slice_in_dim(out, got, lax.rem(me - amount + size, size) * step, 0)
    return out


def local(queries, query_slots, w_res, labels, blocks, positives):
    y = lax.axis_index("y")
    z = lax.axis_index("z")
    me = y * NZ + z
    group = lax.axis_index("x") * lax.axis_size("core") + lax.axis_index("core")
    devices = lax.axis_size("x") * lax.axis_size("core") * NDEV
    place = jnp.stack([y, z]).astype(jnp.int32)

    here = blocks - group * GRP_BLOCKS
    holder = here // BLK_DEV
    wanted = jnp.max(jnp.where(holder == me, here % BLK_DEV, -1), axis=1)
    columns = jnp.arange(NY, dtype=jnp.int32) * NZ + z
    table = jnp.max(
        jnp.where(holder[:, None, :] == columns[None, :, None], here[:, None, :], -1), axis=2
    ).reshape(-1)

    own_slots = lax.dynamic_slice_in_dim(query_slots, me * ROWS, ROWS)
    owner = own_slots // ROWS
    at = jnp.arange(ROWS, dtype=jnp.int32)
    rank = jnp.sum((owner[:, None] == owner[None, :]) & (at[:, None] < at[None, :]), axis=0)
    spot = owner * PER + rank
    sorter = (spot[None, :] == at[:, None]).astype(BF16)
    outbound = jnp.dot(sorter, queries, preferred_element_type=F32).astype(BF16)
    arrived = lax.all_to_all(
        outbound.reshape(NDEV, PER, D), ("y", "z"), split_axis=0, concat_axis=0, tiled=True
    ).reshape(ROWS, D)

    down, up, far_a, far_b = pack(wanted, place, labels)
    far_a = shift(far_a, "y", 1)
    far_b = shift(far_b, "y", -1)
    prev = shift(up, "y", 1)
    nxt = shift(down, "y", -1)
    far_a = shift(far_a, "y", 1)
    far_b = shift(far_b, "y", -1)

    grid = query_slots.reshape(NDEV, ROWS)
    mine = grid // ROWS == me
    lower = (at[:, None] < at[None, :]).astype(BF16)
    before = jnp.dot(mine.astype(BF16), lower, preferred_element_type=F32).astype(jnp.int32)
    turn = jnp.arange(PER, dtype=jnp.int32)
    chosen = mine[:, None, :] & (before[:, None, :] == turn[None, :, None])
    incoming = jnp.sum(
        jnp.where(chosen, (grid - me * ROWS)[:, None, :], 0), axis=2
    ).reshape(ROWS)
    arrange = (incoming[None, :] == at[:, None]).astype(BF16)
    clustered_queries = jnp.dot(arrange, arrived, preferred_element_type=F32).astype(BF16)
    pre = jnp.dot(clustered_queries, w_res, preferred_element_type=F32)
    hidden = (clustered_queries.astype(F32) + activate(pre)).astype(BF16)

    label_at = positives - group * (GRP_BLOCKS * BLK)
    coded = jnp.stack([label_at // 16384, (label_at // 128) % 128, label_at % 128], axis=2)
    coded = jnp.pad(coded.reshape(ROWS, 3 * NPOS), ((0, 0), (0, ENC - 3 * NPOS))).astype(BF16)
    gathered = lax.all_gather(
        jnp.concatenate([hidden, coded], axis=1), "z", axis=0, tiled=True
    )

    grads, part0, part1, part2a, part2b, part3, loss = meet(
        table, wanted, place, gathered, labels, nxt, far_a, far_b, prev
    )

    lead = shift(grads[4, :CSIZE].astype(BF16), "z", 1)
    trail = shift(grads[4, CSIZE:].astype(BF16), "z", -1)
    lead = jnp.concatenate([lead.astype(F32) + grads[3, :CSIZE], grads[3, CSIZE:]])
    trail = jnp.concatenate([grads[5, :CSIZE], trail.astype(F32) + grads[5, CSIZE:]])
    for hop in (2, 1):
        lead = shift(lead.astype(BF16), "z", 1).astype(F32) + grads[hop]
        trail = shift(trail.astype(BF16), "z", -1).astype(F32) + grads[NZ - hop]
    lead = shift(lead.astype(BF16), "z", 1).astype(F32)
    trail = shift(trail.astype(BF16), "z", -1).astype(F32)
    hidden_grad = (lead + trail + grads[0]).astype(BF16)

    back1 = shift(part1, "y", 1)
    back3 = shift(part3, "y", -1)
    back2a = shift(shift(part2a, "y", 1), "y", 1)
    back2b = shift(shift(part2b, "y", -1), "y", -1)

    pre_grad = (hidden_grad.astype(F32) * activate_slope(pre)).astype(BF16)
    back = lax.dot_general(
        pre_grad, w_res, (((1,), (1,)), ((), ())), preferred_element_type=F32
    )
    query_rows = (hidden_grad.astype(F32) + back).astype(BF16)
    term = lax.dot_general(
        clustered_queries, pre_grad, (((0,), (0,)), ((), ())), preferred_element_type=F32
    )
    term = scatter_sum(term, "core")
    term = scatter_sum(term, "x")
    term = scatter_sum(term, "y")
    whole = term
    for amount in range(1, NZ):
        whole = whole + shift(term, "z", amount)
    weight = (whole * float(ROWS * devices) ** (-0.5)).astype(BF16)
    weight = gather_rows(weight, "y")
    weight = gather_rows(weight, "x")
    weight = gather_rows(weight, "core")

    returning = lax.dot_general(
        arrange, query_rows, (((0,), (0,)), ((), ())), preferred_element_type=F32
    ).astype(BF16)
    returned = lax.all_to_all(
        returning.reshape(NDEV, PER, D), ("y", "z"), split_axis=0, concat_axis=0, tiled=True
    ).reshape(ROWS, D)
    query_grad = lax.dot_general(
        sorter, returned, (((0,), (0,)), ((), ())), preferred_element_type=F32
    ).astype(BF16)

    label_grad = fold(wanted, place, part0, back3, back2a, back2b, back1)
    losses = lax.all_gather(loss, "z", axis=0)
    query_loss = jnp.sum(
        lax.dynamic_slice_in_dim(losses, z, 1, 1)[:, 0], axis=0
    ) / float(SHORT * BLK)
    return query_loss, query_grad, label_grad, weight


def solution(mesh):
    inner = Mesh(
        mesh.devices.reshape(mesh.shape["grp"] // 2, 2, NY, NZ), ("x", "core", "y", "z")
    )
    every = ("x", "core", "y", "z")
    group = ("x", "core")
    in_specs = (
        P(every, None), P(group), P(), P(every, None, None), P(group, None), P(every, None),
    )
    out_specs = (P(every), P(every, None), P(every, None, None), P())
    return jax.shard_map(
        local, mesh=inner, in_specs=in_specs, out_specs=out_specs, check_vma=False
    )
```

```python
import jax
import jax.numpy as jnp
from jax import lax
from jax.experimental import pallas as pl
from jax.experimental.pallas import tpu as pltpu
from jax.sharding import Mesh, PartitionSpec as P


D = 768
HALF = D // 2
BLK = 128
CSIZE = 128
SHORT = 12
NPOS = 4
BLK_DEV = 20
ENC = 128
NY = 4
NZ = 8
NDEV = NY * NZ
ROWS = 2 * CSIZE
PER = ROWS // NDEV
GRP_BLOCKS = NDEV * BLK_DEV

F32 = jnp.float32
BF16 = jnp.bfloat16

TALL = ROWS + 8


def activate(values):
    return jax.nn.gelu(values, approximate=True)


def activate_slope(values):
    return jax.vjp(activate, values)[1](jnp.ones_like(values))[0]


def wanted_of(wanted_ref, y, delta, zo):
    owner = lax.rem(y + delta, NY) * NZ + zo
    return jnp.maximum(wanted_ref[2 * owner], wanted_ref[2 * owner + 1])


def pack_kernel(wanted_ref, place_ref, labels, down, up, far_a, far_b, held, in_sem, out_sem):
    y = place_ref[0]
    ins = []
    for slot in range(3 * NZ):
        delta = (NY - 1, 1, 2)[slot // NZ]
        pick = jnp.maximum(wanted_of(wanted_ref, y, delta, slot % NZ), 0)
        copy = pltpu.make_async_copy(labels.at[pick], held.at[slot], in_sem.at[slot])
        copy.start()
        ins.append(copy)
    order = list(range(2 * NZ, 3 * NZ)) + list(range(2 * NZ))
    outs = []
    for slot in order:
        ins[slot].wait()
        zo = slot % NZ
        if slot < 2 * NZ:
            target = (down, up)[slot // NZ]
            moves = [pltpu.make_async_copy(held.at[slot], target.at[zo], out_sem.at[slot])]
        else:
            moves = [
                pltpu.make_async_copy(
                    held.at[slot, :, pl.ds(0, HALF)], far_a.at[zo], out_sem.at[slot]
                ),
                pltpu.make_async_copy(
                    held.at[slot, :, pl.ds(HALF, HALF)], far_b.at[zo], out_sem.at[slot + NZ]
                ),
            ]
        for move in moves:
            move.start()
        outs.extend(moves)
    for move in outs:
        move.wait()


def pack(wanted, place, labels):
    any_spec = pl.BlockSpec(memory_space=pl.ANY)
    full = jax.ShapeDtypeStruct((NZ, BLK, D), BF16)
    half = jax.ShapeDtypeStruct((NZ, BLK, HALF), BF16)
    return pl.pallas_call(
        pack_kernel,
        out_shape=(full, full, half, half),
        grid_spec=pltpu.PrefetchScalarGridSpec(
            num_scalar_prefetch=2,
            grid=(1,),
            in_specs=[any_spec],
            out_specs=[any_spec] * 4,
            scratch_shapes=[
                pltpu.VMEM((3 * NZ, BLK, D), BF16),
                pltpu.SemaphoreType.DMA((3 * NZ,)),
                pltpu.SemaphoreType.DMA((4 * NZ,)),
            ],
        ),
        cost_estimate=pl.CostEstimate(flops=0, bytes_accessed=10_000_000, transcendentals=0),
        name="pack",
    )(wanted, place, labels)


def meet_kernel(
    table_ref, wanted_ref, place_ref,
    rows_ref, own_ref, next_ref, far_a_ref, far_b_ref, prev_ref,
    grad_ref, part0_ref, part1_ref, part2a_ref, part2b_ref, part3_ref,
    labs,
):
    y = place_ref[0]
    z = place_ref[1]
    zo = lax.rem(z + pl.program_id(0), NZ)
    rows = rows_ref[:, :D]
    coded = rows_ref[:, D:].astype(F32)
    ids = [
        coded[:, 3 * n : 3 * n + 1] * 16384.0
        + coded[:, 3 * n + 1 : 3 * n + 2] * 128.0
        + coded[:, 3 * n + 2 : 3 * n + 3]
        for n in range(NPOS)
    ]
    labs[0:BLK, :] = own_ref[0]
    labs[BLK : 2 * BLK, :] = next_ref[0]
    labs[2 * BLK : 3 * BLK, :HALF] = far_a_ref[0]
    labs[2 * BLK : 3 * BLK, HALF:] = far_b_ref[0]
    labs[3 * BLK : 4 * BLK, :] = prev_ref[0]
    blocks_here = labs[...]
    logits = lax.dot_general(
        rows, blocks_here, (((1,), (1,)), ((), ())), preferred_element_type=F32
    )
    row_at = lax.broadcasted_iota(jnp.int32, (ROWS, BLK), 0)
    lane_at = lax.broadcasted_iota(jnp.int32, (ROWS, BLK), 1).astype(F32)
    loss = jnp.zeros((ROWS, BLK), F32)
    errors = []
    for delta in range(NY):
        holder_y = lax.rem(y + delta, NY)
        base = (y * NZ + zo) * 2 * NY + holder_y
        first = table_ref[base]
        second = table_ref[base + NY]
        block = (jnp.maximum(first, second) * BLK).astype(F32)
        live = jnp.where(row_at < CSIZE, first, second) >= 0
        here = logits[:, delta * BLK : (delta + 1) * BLK]
        hit = jnp.zeros((ROWS, BLK), jnp.bool_)
        for n in range(NPOS):
            hit = jnp.logical_or(hit, (ids[n] - block) == lane_at)
        targets = hit.astype(F32)
        tail = jnp.exp(-jnp.abs(here))
        soft = jnp.maximum(here, 0.0) + jnp.log1p(tail)
        sig = jnp.where(here >= 0, 1.0, tail) / (1.0 + tail)
        loss += jnp.where(live, soft - targets * here, 0.0)
        errors.append(jnp.where(live, sig - targets, 0.0).astype(BF16))
    errors = jnp.concatenate(errors, axis=1)
    grad_ref[0, :ROWS] = jnp.dot(errors, blocks_here, preferred_element_type=F32)
    parts = lax.dot_general(
        errors, rows, (((0,), (0,)), ((), ())), preferred_element_type=F32
    ).astype(BF16)
    part0_ref[0] = parts[0:BLK]
    part1_ref[0] = parts[BLK : 2 * BLK]
    part2a_ref[0] = parts[2 * BLK : 3 * BLK, :HALF]
    part2b_ref[0] = parts[2 * BLK : 3 * BLK, HALF:]
    part3_ref[0] = parts[3 * BLK : 4 * BLK]
    sums = lax.dot_general(
        jnp.ones((8, BLK), F32), loss, (((1,), (1,)), ((), ())),
        precision=lax.Precision.HIGHEST, preferred_element_type=F32,
    )
    grad_ref[0, ROWS:] = jnp.concatenate([sums, jnp.zeros((8, D - ROWS), F32)], axis=1)


def meet(table, wanted, place, gathered, labels, nxt, far_a, far_b, prev):
    def owner_of(i, place_ref):
        return lax.rem(place_ref[1] + i, NZ)

    def own_map(i, table_ref, wanted_ref, place_ref):
        pick = wanted_of(wanted_ref, place_ref[0], 0, owner_of(i, place_ref))
        return (jnp.maximum(pick, 0), 0, 0)

    def owner_map(i, table_ref, wanted_ref, place_ref):
        return (owner_of(i, place_ref), 0, 0)

    full = pl.BlockSpec((1, BLK, D), owner_map)
    half = pl.BlockSpec((1, BLK, HALF), owner_map)
    full_shape = jax.ShapeDtypeStruct((NZ, BLK, D), BF16)
    half_shape = jax.ShapeDtypeStruct((NZ, BLK, HALF), BF16)
    return pl.pallas_call(
        meet_kernel,
        out_shape=(
            jax.ShapeDtypeStruct((NZ, TALL, D), F32),
            full_shape, full_shape, half_shape, half_shape, full_shape,
        ),
        grid_spec=pltpu.PrefetchScalarGridSpec(
            num_scalar_prefetch=3,
            grid=(NZ,),
            in_specs=[
                pl.BlockSpec((ROWS, D + ENC), lambda i, t, w, p: (owner_of(i, p), 0)),
                pl.BlockSpec((1, BLK, D), own_map),
                full, half, half, full,
            ],
            out_specs=[
                pl.BlockSpec((1, TALL, D), lambda i, t, w, p: (i, 0, 0)),
                full, full, half, half, full,
            ],
            scratch_shapes=[pltpu.VMEM((NY * BLK, D), BF16)],
        ),
        cost_estimate=pl.CostEstimate(
            flops=5_000_000_000, bytes_accessed=25_000_000, transcendentals=3_000_000
        ),
        name="meet",
    )(table, wanted, place, gathered, labels, nxt, far_a, far_b, prev)


def fold_kernel(wanted_ref, place_ref, own, up, far_a, far_b, down, out, total):
    y = place_ref[0]
    total[...] = jnp.zeros_like(total)

    def one(zo, carry):
        for delta in range(NY):
            pick = wanted_of(wanted_ref, y, delta, zo)

            @pl.when(pick >= 0)
            def _():
                if delta == 2:
                    total[pick, :, :HALF] += far_a[zo].astype(F32)
                    total[pick, :, HALF:] += far_b[zo].astype(F32)
                else:
                    total[pick] += (own, up, None, down)[delta][zo].astype(F32)

        return carry

    lax.fori_loop(0, NZ, one, 0)

    def put(b, carry):
        out[b] = total[b].astype(BF16)
        return carry

    lax.fori_loop(0, BLK_DEV, put, 0)


def fold(wanted, place, own, up, far_a, far_b, down):
    vmem = pl.BlockSpec(memory_space=pltpu.VMEM)
    return pl.pallas_call(
        fold_kernel,
        out_shape=jax.ShapeDtypeStruct((BLK_DEV, BLK, D), BF16),
        grid_spec=pltpu.PrefetchScalarGridSpec(
            num_scalar_prefetch=2,
            grid=(1,),
            in_specs=[
                pl.BlockSpec((NZ, BLK, D), lambda i, w, p: (0, 0, 0)),
                pl.BlockSpec((NZ, BLK, D), lambda i, w, p: (0, 0, 0)),
                pl.BlockSpec((NZ, BLK, HALF), lambda i, w, p: (0, 0, 0)),
                pl.BlockSpec((NZ, BLK, HALF), lambda i, w, p: (0, 0, 0)),
                pl.BlockSpec((NZ, BLK, D), lambda i, w, p: (0, 0, 0)),
            ],
            out_specs=pl.BlockSpec((BLK_DEV, BLK, D), lambda i, w, p: (0, 0, 0)),
            scratch_shapes=[pltpu.VMEM((BLK_DEV, BLK, D), F32)],
        ),
        cost_estimate=pl.CostEstimate(flops=5_000_000, bytes_accessed=25_000_000, transcendentals=0),
        compiler_params=pltpu.CompilerParams(vmem_limit_bytes=48 * 1024 * 1024),
        name="fold",
    )(wanted, place, own, up, far_a, far_b, down)


def shift(values, axis, amount):
    size = lax.axis_size(axis)
    return lax.ppermute(values, axis, [(i, (i + amount) % size) for i in range(size)])


def scatter_sum(values, axis):
    size = lax.axis_size(axis)
    me = lax.axis_index(axis)
    step = values.shape[0] // size

    def piece(amount):
        at = lax.rem(me + amount, size) * step
        return lax.dynamic_slice_in_dim(values, at, step, 0)

    total = piece(0)
    for got in [shift(piece(amount), axis, amount) for amount in range(1, size)]:
        total = total + got
    return total


def gather_rows(values, axis):
    size = lax.axis_size(axis)
    me = lax.axis_index(axis)
    step = values.shape[0]
    out = jnp.zeros((size * step,) + values.shape[1:], values.dtype)
    out = lax.dynamic_update_slice_in_dim(out, values, me * step, 0)
    for amount in range(1, size):
        got = shift(values, axis, amount)
        out = lax.dynamic_update_slice_in_dim(out, got, lax.rem(me - amount + size, size) * step, 0)
    return out


def step(queries, query_slots, w_res, labels, blocks, positives):
    y = lax.axis_index("y")
    z = lax.axis_index("z")
    me = y * NZ + z
    group = lax.axis_index("x") * lax.axis_size("core") + lax.axis_index("core")
    devices = lax.axis_size("x") * lax.axis_size("core") * NDEV
    place = jnp.stack([y, z]).astype(jnp.int32)

    here = blocks - group * GRP_BLOCKS
    holder = here // BLK_DEV
    wanted = jnp.max(jnp.where(holder == me, here % BLK_DEV, -1), axis=1)
    columns = jnp.arange(NY, dtype=jnp.int32) * NZ + z
    table = jnp.max(
        jnp.where(holder[:, None, :] == columns[None, :, None], here[:, None, :], -1), axis=2
    ).reshape(-1)

    own_slots = lax.dynamic_slice_in_dim(query_slots, me * ROWS, ROWS)
    owner = own_slots // ROWS
    at = jnp.arange(ROWS, dtype=jnp.int32)
    rank = jnp.sum((owner[:, None] == owner[None, :]) & (at[:, None] < at[None, :]), axis=0)
    spot = owner * PER + rank
    sorter = (spot[None, :] == at[:, None]).astype(BF16)
    outbound = jnp.dot(sorter, queries, preferred_element_type=F32).astype(BF16)
    down, up, far_a, far_b = pack(wanted, place, labels)
    arrived = lax.all_to_all(
        outbound.reshape(NDEV, PER, D), ("y", "z"), split_axis=0, concat_axis=0, tiled=True
    )
    arrived, _ = lax.optimization_barrier((arrived, far_a))
    arrived = arrived.reshape(ROWS, D)

    far_a = shift(far_a, "y", 1)
    far_b = shift(far_b, "y", -1)
    prev = shift(up, "y", 1)
    nxt = shift(down, "y", -1)
    far_a = shift(far_a, "y", 1)
    far_b = shift(far_b, "y", -1)

    grid = query_slots.reshape(NDEV, ROWS)
    mine = grid // ROWS == me
    lower = (at[:, None] < at[None, :]).astype(BF16)
    before = jnp.dot(mine.astype(BF16), lower, preferred_element_type=F32).astype(jnp.int32)
    turn = jnp.arange(PER, dtype=jnp.int32)
    chosen = mine[:, None, :] & (before[:, None, :] == turn[None, :, None])
    incoming = jnp.sum(
        jnp.where(chosen, (grid - me * ROWS)[:, None, :], 0), axis=2
    ).reshape(ROWS)
    arrange = (incoming[None, :] == at[:, None]).astype(BF16)
    clustered_queries = jnp.dot(arrange, arrived, preferred_element_type=F32).astype(BF16)
    pre = jnp.dot(clustered_queries, w_res, preferred_element_type=F32)
    hidden = (clustered_queries.astype(F32) + activate(pre)).astype(BF16)

    label_at = positives - group * (GRP_BLOCKS * BLK)
    coded = jnp.stack([label_at // 16384, (label_at // 128) % 128, label_at % 128], axis=2)
    coded = jnp.pad(coded.reshape(ROWS, 3 * NPOS), ((0, 0), (0, ENC - 3 * NPOS))).astype(BF16)
    gathered = lax.all_gather(
        jnp.concatenate([hidden, coded], axis=1), "z", axis=0, tiled=True
    )

    grads, part0, part1, part2a, part2b, part3 = meet(
        table, wanted, place, gathered, labels, nxt, far_a, far_b, prev
    )

    back2a = shift(part2a, "y", 1)
    back2b = shift(part2b, "y", -1)
    back1 = shift(part1, "y", 1)
    back3 = shift(part3, "y", -1)
    back2a = shift(back2a, "y", 1)
    back2b = shift(back2b, "y", -1)

    lead = shift(grads[4, :CSIZE].astype(BF16), "z", 1)
    trail = shift(grads[4, CSIZE:].astype(BF16), "z", -1)
    lead = jnp.concatenate([lead.astype(F32) + grads[3, :CSIZE], grads[3, CSIZE:]])
    trail = jnp.concatenate([grads[5, :CSIZE], trail.astype(F32) + grads[5, CSIZE:]])
    for hop in (2, 1):
        lead = shift(lead.astype(BF16), "z", 1).astype(F32) + grads[hop]
        trail = shift(trail.astype(BF16), "z", -1).astype(F32) + grads[NZ - hop]
    lead = shift(lead.astype(BF16), "z", 1).astype(F32)
    trail = shift(trail.astype(BF16), "z", -1).astype(F32)
    summed = lead + trail + grads[0]
    hidden_grad = summed[:ROWS].astype(BF16)
    query_loss = summed[ROWS, :ROWS] / float(SHORT * BLK)

    pre_grad = (hidden_grad.astype(F32) * activate_slope(pre)).astype(BF16)
    back = lax.dot_general(
        pre_grad, w_res, (((1,), (1,)), ((), ())), preferred_element_type=F32
    )
    query_rows = (hidden_grad.astype(F32) + back).astype(BF16)
    term = lax.dot_general(
        clustered_queries, pre_grad, (((0,), (0,)), ((), ())), preferred_element_type=F32
    )
    term = scatter_sum(term, "core")
    term = scatter_sum(term, "x")
    term = scatter_sum(term, "y")
    whole = term
    for amount in range(1, NZ):
        whole = whole + shift(term, "z", amount)
    weight = (whole * float(ROWS * devices) ** (-0.5)).astype(BF16)
    weight = gather_rows(weight, "y")
    weight = gather_rows(weight, "x")
    weight = gather_rows(weight, "core")

    returning = lax.dot_general(
        arrange, query_rows, (((0,), (0,)), ((), ())), preferred_element_type=F32
    ).astype(BF16)
    returned = lax.all_to_all(
        returning.reshape(NDEV, PER, D), ("y", "z"), split_axis=0, concat_axis=0, tiled=True
    ).reshape(ROWS, D)
    query_grad = lax.dot_general(
        sorter, returned, (((0,), (0,)), ((), ())), preferred_element_type=F32
    ).astype(BF16)

    label_grad = fold(wanted, place, part0, back3, back2a, back2b, back1)
    return query_loss, query_grad, label_grad, weight


def solution(mesh):
    inner = Mesh(
        mesh.devices.reshape(mesh.shape["grp"] // 2, 2, NY, NZ), ("x", "core", "y", "z")
    )
    every = ("x", "core", "y", "z")
    group = ("x", "core")
    in_specs = (
        P(every, None), P(group), P(), P(every, None, None), P(group, None), P(every, None),
    )
    out_specs = (P(every), P(every, None), P(every, None, None), P())
    return jax.shard_map(step, mesh=inner, in_specs=in_specs, out_specs=out_specs, check_vma=False)
```

```python
import functools

import jax
import jax.numpy as jnp
from jax import lax
from jax.experimental import pallas as pl
from jax.experimental.pallas import tpu as pltpu
from jax.sharding import Mesh, PartitionSpec as P


D = 768
HALF = D // 2
BLK = 128
CSIZE = 128
SHORT = 12
NPOS = 4
BLK_DEV = 20
ENC = 128
NY = 4
NZ = 8
NDEV = NY * NZ
ROWS = 2 * CSIZE
PER = ROWS // NDEV
GRP_BLOCKS = NDEV * BLK_DEV

F32 = jnp.float32
BF16 = jnp.bfloat16

TALL = ROWS + 8


def activate(values):
    return jax.nn.gelu(values, approximate=True)


def activate_slope(values):
    return jax.vjp(activate, values)[1](jnp.ones_like(values))[0]


def wanted_of(wanted_ref, y, delta, zo):
    owner = lax.rem(y + delta, NY) * NZ + zo
    return jnp.maximum(wanted_ref[2 * owner], wanted_ref[2 * owner + 1])


def pack_kernel(wanted_ref, place_ref, labels, down, up, far_a, far_b, held, in_sem, out_sem):
    y = place_ref[0]
    ins = []
    for slot in range(3 * NZ):
        delta = (NY - 1, 1, 2)[slot // NZ]
        pick = jnp.maximum(wanted_of(wanted_ref, y, delta, slot % NZ), 0)
        copy = pltpu.make_async_copy(labels.at[pick], held.at[slot], in_sem.at[slot])
        copy.start()
        ins.append(copy)
    order = list(range(2 * NZ, 3 * NZ)) + list(range(2 * NZ))
    outs = []
    for slot in order:
        ins[slot].wait()
        zo = slot % NZ
        if slot < 2 * NZ:
            target = (down, up)[slot // NZ]
            moves = [pltpu.make_async_copy(held.at[slot], target.at[zo], out_sem.at[slot])]
        else:
            moves = [
                pltpu.make_async_copy(
                    held.at[slot, :, pl.ds(0, HALF)], far_a.at[zo], out_sem.at[slot]
                ),
                pltpu.make_async_copy(
                    held.at[slot, :, pl.ds(HALF, HALF)], far_b.at[zo], out_sem.at[slot + NZ]
                ),
            ]
        for move in moves:
            move.start()
        outs.extend(moves)
    for move in outs:
        move.wait()


def pack(wanted, place, labels):
    any_spec = pl.BlockSpec(memory_space=pl.ANY)
    full = jax.ShapeDtypeStruct((NZ, BLK, D), BF16)
    half = jax.ShapeDtypeStruct((NZ, BLK, HALF), BF16)
    return pl.pallas_call(
        pack_kernel,
        out_shape=(full, full, half, half),
        grid_spec=pltpu.PrefetchScalarGridSpec(
            num_scalar_prefetch=2,
            grid=(1,),
            in_specs=[any_spec],
            out_specs=[any_spec] * 4,
            scratch_shapes=[
                pltpu.VMEM((3 * NZ, BLK, D), BF16),
                pltpu.SemaphoreType.DMA((3 * NZ,)),
                pltpu.SemaphoreType.DMA((4 * NZ,)),
            ],
        ),
        cost_estimate=pl.CostEstimate(flops=0, bytes_accessed=10_000_000, transcendentals=0),
        name="pack",
    )(wanted, place, labels)


def meet_kernel(
    leading, carried,
    table_ref, wanted_ref, place_ref,
    rows_ref, own_ref, next_ref, far_a_ref, far_b_ref, prev_ref,
    *refs,
):
    refs = refs[carried:]
    part0_ref, part1_ref, part2a_ref, part2b_ref, part3_ref, grad_ref = refs[:6]
    labs = refs[-1]
    y = place_ref[0]
    zo = place_ref[2 + pl.program_id(0)]
    rows = rows_ref[:, :D]
    coded = rows_ref[:, D:].astype(F32)
    ids = [
        coded[:, 3 * n : 3 * n + 1] * 16384.0
        + coded[:, 3 * n + 1 : 3 * n + 2] * 128.0
        + coded[:, 3 * n + 2 : 3 * n + 3]
        for n in range(NPOS)
    ]
    labs[0:BLK, :] = own_ref[0]
    labs[BLK : 2 * BLK, :] = next_ref[0]
    labs[2 * BLK : 3 * BLK, :HALF] = far_a_ref[0]
    labs[2 * BLK : 3 * BLK, HALF:] = far_b_ref[0]
    labs[3 * BLK : 4 * BLK, :] = prev_ref[0]
    blocks_here = labs[...]
    logits = lax.dot_general(
        rows, blocks_here, (((1,), (1,)), ((), ())), preferred_element_type=F32
    )
    row_at = lax.broadcasted_iota(jnp.int32, (ROWS, BLK), 0)
    lane_at = lax.broadcasted_iota(jnp.int32, (ROWS, BLK), 1).astype(F32)
    loss = jnp.zeros((ROWS, BLK), F32)
    errors = []
    for delta in range(NY):
        holder_y = lax.rem(y + delta, NY)
        base = (y * NZ + zo) * 2 * NY + holder_y
        first = table_ref[base]
        second = table_ref[base + NY]
        block = (jnp.maximum(first, second) * BLK).astype(F32)
        live = jnp.where(row_at < CSIZE, first, second) >= 0
        here = logits[:, delta * BLK : (delta + 1) * BLK]
        hit = jnp.zeros((ROWS, BLK), jnp.bool_)
        for n in range(NPOS):
            hit = jnp.logical_or(hit, (ids[n] - block) == lane_at)
        targets = hit.astype(F32)
        tail = jnp.exp(-jnp.abs(here))
        soft = jnp.maximum(here, 0.0) + jnp.log1p(tail)
        sig = jnp.where(here >= 0, 1.0, tail) / (1.0 + tail)
        loss += jnp.where(live, soft - targets * here, 0.0)
        errors.append(jnp.where(live, sig - targets, 0.0).astype(BF16))
    errors = jnp.concatenate(errors, axis=1)
    grad = jnp.dot(errors, blocks_here, preferred_element_type=F32)
    parts = lax.dot_general(
        errors, rows, (((0,), (0,)), ((), ())), preferred_element_type=F32
    ).astype(BF16)
    part0_ref[0] = parts[0:BLK]
    part1_ref[0] = parts[BLK : 2 * BLK]
    part2a_ref[0] = parts[2 * BLK : 3 * BLK, :HALF]
    part2b_ref[0] = parts[2 * BLK : 3 * BLK, HALF:]
    part3_ref[0] = parts[3 * BLK : 4 * BLK]
    sums = lax.dot_general(
        jnp.ones((8, BLK), F32), loss, (((1,), (1,)), ((), ())),
        precision=lax.Precision.HIGHEST, preferred_element_type=F32,
    )
    extra = jnp.concatenate([sums, jnp.zeros((8, D - ROWS), F32)], axis=1)

    def keep():
        grad_ref[0, :ROWS] = grad
        grad_ref[0, ROWS:] = extra

    if leading:
        lead_ref, trail_ref = refs[6:8]

        @pl.when(pl.program_id(0) == 0)
        def _():
            lead_ref[...] = grad[:CSIZE].astype(BF16)
            trail_ref[:CSIZE] = grad[CSIZE:].astype(BF16)
            trail_ref[CSIZE:] = extra.astype(BF16)

        pl.when(pl.program_id(0) > 0)(keep)
    else:
        keep()


def meet(offsets, table, wanted, y, z, gathered, labels, nxt, far_a, far_b, prev, parts=()):
    leading = not parts
    count = len(offsets)
    turns = offsets + offsets[-1:] * (6 - count)
    place = jnp.stack([y, z] + [(z + offset) % NZ for offset in turns]).astype(jnp.int32)

    def own_map(i, table_ref, wanted_ref, place_ref):
        pick = wanted_of(wanted_ref, place_ref[0], 0, place_ref[2 + i])
        return (jnp.maximum(pick, 0), 0, 0)

    def owner_map(i, table_ref, wanted_ref, place_ref):
        return (place_ref[2 + i], 0, 0)

    def grad_map(i, table_ref, wanted_ref, place_ref):
        return (jnp.maximum(i - 1, 0) if leading else i, 0, 0)

    full = pl.BlockSpec((1, BLK, D), owner_map)
    half = pl.BlockSpec((1, BLK, HALF), owner_map)
    full_shape = jax.ShapeDtypeStruct((NZ, BLK, D), BF16)
    half_shape = jax.ShapeDtypeStruct((NZ, BLK, HALF), BF16)
    out_shape = [full_shape, full_shape, half_shape, half_shape, full_shape]
    out_shape.append(jax.ShapeDtypeStruct((count - leading, TALL, D), F32))
    out_specs = [full, full, half, half, full, pl.BlockSpec((1, TALL, D), grad_map)]
    if leading:
        for tall in (CSIZE, TALL - CSIZE):
            out_shape.append(jax.ShapeDtypeStruct((tall, D), BF16))
            out_specs.append(pl.BlockSpec((tall, D), lambda i, t, w, p: (0, 0)))
    return pl.pallas_call(
        functools.partial(meet_kernel, leading, len(parts)),
        out_shape=tuple(out_shape),
        grid_spec=pltpu.PrefetchScalarGridSpec(
            num_scalar_prefetch=3,
            grid=(count,),
            in_specs=[
                pl.BlockSpec((ROWS, D + ENC), lambda i, t, w, p: (p[2 + i], 0)),
                pl.BlockSpec((1, BLK, D), own_map),
                full, half, half, full,
            ] + [pl.BlockSpec(memory_space=pl.ANY)] * len(parts),
            out_specs=out_specs,
            scratch_shapes=[pltpu.VMEM((NY * BLK, D), BF16)],
        ),
        input_output_aliases={9 + n: n for n in range(len(parts))},
        cost_estimate=pl.CostEstimate(
            flops=600_000_000 * count, bytes_accessed=3_000_000 * count,
            transcendentals=400_000 * count,
        ),
        name="meet",
    )(table, wanted, place, gathered, labels, nxt, far_a, far_b, prev, *parts)


def fold_kernel(wanted_ref, place_ref, own, up, far_a, far_b, down, out, total):
    y = place_ref[0]
    total[...] = jnp.zeros_like(total)

    def one(zo, carry):
        for delta in range(NY):
            pick = wanted_of(wanted_ref, y, delta, zo)

            @pl.when(pick >= 0)
            def _():
                if delta == 2:
                    total[pick, :, :HALF] += far_a[zo].astype(F32)
                    total[pick, :, HALF:] += far_b[zo].astype(F32)
                else:
                    total[pick] += (own, up, None, down)[delta][zo].astype(F32)

        return carry

    lax.fori_loop(0, NZ, one, 0)

    def put(b, carry):
        out[b] = total[b].astype(BF16)
        return carry

    lax.fori_loop(0, BLK_DEV, put, 0)


def fold(wanted, place, own, up, far_a, far_b, down):
    vmem = pl.BlockSpec(memory_space=pltpu.VMEM)
    return pl.pallas_call(
        fold_kernel,
        out_shape=jax.ShapeDtypeStruct((BLK_DEV, BLK, D), BF16),
        grid_spec=pltpu.PrefetchScalarGridSpec(
            num_scalar_prefetch=2,
            grid=(1,),
            in_specs=[
                pl.BlockSpec((NZ, BLK, D), lambda i, w, p: (0, 0, 0)),
                pl.BlockSpec((NZ, BLK, D), lambda i, w, p: (0, 0, 0)),
                pl.BlockSpec((NZ, BLK, HALF), lambda i, w, p: (0, 0, 0)),
                pl.BlockSpec((NZ, BLK, HALF), lambda i, w, p: (0, 0, 0)),
                pl.BlockSpec((NZ, BLK, D), lambda i, w, p: (0, 0, 0)),
            ],
            out_specs=pl.BlockSpec((BLK_DEV, BLK, D), lambda i, w, p: (0, 0, 0)),
            scratch_shapes=[pltpu.VMEM((BLK_DEV, BLK, D), F32)],
        ),
        cost_estimate=pl.CostEstimate(flops=5_000_000, bytes_accessed=25_000_000, transcendentals=0),
        compiler_params=pltpu.CompilerParams(vmem_limit_bytes=48 * 1024 * 1024),
        name="fold",
    )(wanted, place, own, up, far_a, far_b, down)


def shift(values, axis, amount):
    size = lax.axis_size(axis)
    return lax.ppermute(values, axis, [(i, (i + amount) % size) for i in range(size)])


def scatter_sum(values, axis):
    size = lax.axis_size(axis)
    me = lax.axis_index(axis)
    step = values.shape[0] // size

    def piece(amount):
        at = lax.rem(me + amount, size) * step
        return lax.dynamic_slice_in_dim(values, at, step, 0)

    total = piece(0)
    for got in [shift(piece(amount), axis, amount) for amount in range(1, size)]:
        total = total + got
    return total


def gather_turns(values, axis):
    size = lax.axis_size(axis)
    return [values] + [shift(values, axis, amount) for amount in range(1, size)]


def spread_kernel(at_ref, *refs):
    sources, out = refs[:-1], refs[-1]
    x = at_ref[0]
    core = at_ref[1]
    y = at_ref[2]
    step = D // (2 * 4 * NY)
    for place, source in enumerate(sources):
        turn_x = place % 4
        side = core if place < 4 else 1 - core
        for turn_y in range(NY):
            to_x = lax.rem(x - turn_x + 4, 4)
            to_y = lax.rem(y - turn_y + NY, NY)
            to = pl.multiple_of(((side * 4 + to_x) * NY + to_y) * step, 8)
            out[pl.ds(to, step), :] = source[turn_y * step : (turn_y + 1) * step, :]


def spread(at, pieces):
    piece = pl.BlockSpec((D // 8, D), lambda i, a: (0, 0))
    return pl.pallas_call(
        spread_kernel,
        out_shape=jax.ShapeDtypeStruct((D, D), BF16),
        grid_spec=pltpu.PrefetchScalarGridSpec(
            num_scalar_prefetch=1,
            grid=(1,),
            in_specs=[piece] * len(pieces),
            out_specs=pl.BlockSpec((D, D), lambda i, a: (0, 0)),
        ),
        cost_estimate=pl.CostEstimate(flops=0, bytes_accessed=2_400_000, transcendentals=0),
        name="spread",
    )(at, *pieces)


def step(queries, query_slots, w_res, labels, blocks, positives):
    y = lax.axis_index("y")
    z = lax.axis_index("z")
    me = y * NZ + z
    group = lax.axis_index("x") * lax.axis_size("core") + lax.axis_index("core")
    devices = lax.axis_size("x") * lax.axis_size("core") * NDEV
    place = jnp.stack([y, z]).astype(jnp.int32)

    here = blocks - group * GRP_BLOCKS
    holder = here // BLK_DEV
    wanted = jnp.max(jnp.where(holder == me, here % BLK_DEV, -1), axis=1)
    columns = jnp.arange(NY, dtype=jnp.int32) * NZ + z
    table = jnp.max(
        jnp.where(holder[:, None, :] == columns[None, :, None], here[:, None, :], -1), axis=2
    ).reshape(-1)

    own_slots = lax.dynamic_slice_in_dim(query_slots, me * ROWS, ROWS)
    owner = own_slots // ROWS
    at = jnp.arange(ROWS, dtype=jnp.int32)
    rank = jnp.sum((owner[:, None] == owner[None, :]) & (at[:, None] < at[None, :]), axis=0)
    spot = owner * PER + rank
    sorter = (spot[None, :] == at[:, None]).astype(BF16)
    outbound = jnp.dot(sorter, queries, preferred_element_type=F32).astype(BF16)
    down, up, far_a, far_b = pack(wanted, place, labels)
    arrived = lax.all_to_all(
        outbound.reshape(NDEV, PER, D), ("y", "z"), split_axis=0, concat_axis=0, tiled=True
    )
    arrived, _ = lax.optimization_barrier((arrived, far_a))
    arrived = arrived.reshape(ROWS, D)

    far_a = shift(far_a, "y", 1)
    far_b = shift(far_b, "y", -1)
    prev = shift(up, "y", 1)
    nxt = shift(down, "y", -1)
    far_a = shift(far_a, "y", 1)
    far_b = shift(far_b, "y", -1)

    grid = query_slots.reshape(NDEV, ROWS)
    mine = grid // ROWS == me
    lower = (at[:, None] < at[None, :]).astype(BF16)
    before = jnp.dot(mine.astype(BF16), lower, preferred_element_type=F32).astype(jnp.int32)
    turn = jnp.arange(PER, dtype=jnp.int32)
    chosen = mine[:, None, :] & (before[:, None, :] == turn[None, :, None])
    incoming = jnp.sum(
        jnp.where(chosen, (grid - me * ROWS)[:, None, :], 0), axis=2
    ).reshape(ROWS)
    arrange = (incoming[None, :] == at[:, None]).astype(BF16)
    clustered_queries = jnp.dot(arrange, arrived, preferred_element_type=F32).astype(BF16)
    pre = jnp.dot(clustered_queries, w_res, preferred_element_type=F32)
    hidden = (clustered_queries.astype(F32) + activate(pre)).astype(BF16)

    label_at = positives - group * (GRP_BLOCKS * BLK)
    coded = jnp.stack([label_at // 16384, (label_at // 128) % 128, label_at % 128], axis=2)
    coded = jnp.pad(coded.reshape(ROWS, 3 * NPOS), ((0, 0), (0, ENC - 3 * NPOS))).astype(BF16)
    gathered = lax.all_gather(
        jnp.concatenate([hidden, coded], axis=1), "z", axis=0, tiled=True
    )

    common = (table, wanted, y, z, gathered, labels, nxt, far_a, far_b, prev)
    *parts, grads_a, lead, trail = meet((4, 3, 5), *common)
    lead = shift(lead, "z", 1)
    trail = shift(trail, "z", -1)
    *parts, grads_b = meet((2, 6), *common, parts=tuple(parts))
    lead = jnp.concatenate([lead.astype(F32) + grads_a[0, :CSIZE], grads_a[0, CSIZE:]])
    trail = jnp.concatenate([grads_a[1, :CSIZE], trail.astype(F32) + grads_a[1, CSIZE:]])
    lead = shift(lead.astype(BF16), "z", 1)
    trail = shift(trail.astype(BF16), "z", -1)
    *parts, grads_c = meet((1, 7, 0), *common, parts=tuple(parts))
    part0, part1, part2a, part2b, part3 = parts

    back2a = shift(part2a, "y", 1)
    back2b = shift(part2b, "y", -1)
    back1 = shift(part1, "y", 1)
    back3 = shift(part3, "y", -1)

    lead = shift((lead.astype(F32) + grads_b[0]).astype(BF16), "z", 1)
    trail = shift((trail.astype(F32) + grads_b[1]).astype(BF16), "z", -1)
    back2a = shift(back2a, "y", 1)
    back2b = shift(back2b, "y", -1)
    lead = shift((lead.astype(F32) + grads_c[0]).astype(BF16), "z", 1)
    trail = shift((trail.astype(F32) + grads_c[1]).astype(BF16), "z", -1)
    summed = lead.astype(F32) + trail.astype(F32) + grads_c[2]
    hidden_grad = summed[:ROWS].astype(BF16)
    query_loss = summed[ROWS, :ROWS] / float(SHORT * BLK)

    pre_grad = (hidden_grad.astype(F32) * activate_slope(pre)).astype(BF16)
    back = lax.dot_general(
        pre_grad, w_res, (((1,), (1,)), ((), ())), preferred_element_type=F32
    )
    query_rows = (hidden_grad.astype(F32) + back).astype(BF16)
    core = lax.axis_index("core")

    def term(side):
        columns = lax.dynamic_slice_in_dim(clustered_queries, side * HALF, HALF, 1)
        return lax.dot_general(
            columns, pre_grad, (((0,), (0,)), ((), ())), preferred_element_type=F32
        )

    other = shift(term(1 - core), "core", 1)
    total = term(core) + other
    total = scatter_sum(total, "x")
    total = scatter_sum(total, "y")
    whole = total
    for amount in range(1, NZ):
        whole = whole + shift(total, "z", amount)
    weight = (whole * float(ROWS * devices) ** (-0.5)).astype(BF16)
    weight = jnp.concatenate(gather_turns(weight, "y"), axis=0)
    pieces = gather_turns(weight, "x")
    pieces = pieces + [shift(piece, "core", 1) for piece in pieces]
    at_here = jnp.stack([lax.axis_index("x"), core, y]).astype(jnp.int32)
    weight = spread(at_here, pieces)

    returning = lax.dot_general(
        arrange, query_rows, (((0,), (0,)), ((), ())), preferred_element_type=F32
    ).astype(BF16)
    returned = lax.all_to_all(
        returning.reshape(NDEV, PER, D), ("y", "z"), split_axis=0, concat_axis=0, tiled=True
    ).reshape(ROWS, D)
    query_grad = lax.dot_general(
        sorter, returned, (((0,), (0,)), ((), ())), preferred_element_type=F32
    ).astype(BF16)

    label_grad = fold(wanted, place, part0, back3, back2a, back2b, back1)
    return query_loss, query_grad, label_grad, weight


def solution(mesh):
    inner = Mesh(
        mesh.devices.reshape(mesh.shape["grp"] // 2, 2, NY, NZ), ("x", "core", "y", "z")
    )
    every = ("x", "core", "y", "z")
    group = ("x", "core")
    in_specs = (
        P(every, None), P(group), P(), P(every, None, None), P(group, None), P(every, None),
    )
    out_specs = (P(every), P(every, None), P(every, None, None), P())
    return jax.shard_map(step, mesh=inner, in_specs=in_specs, out_specs=out_specs, check_vma=False)
```

```python
import functools

import jax
import jax.numpy as jnp
from jax import lax
from jax.experimental import pallas as pl
from jax.experimental.pallas import tpu as pltpu
from jax.sharding import Mesh, PartitionSpec as P


D = 768
HALF = D // 2
BLK = 128
CSIZE = 128
SHORT = 12
NPOS = 4
BLK_DEV = 20
ENC = 128
NY = 4
NZ = 8
NDEV = NY * NZ
ROWS = 2 * CSIZE
PER = ROWS // NDEV
GRP_BLOCKS = NDEV * BLK_DEV

F32 = jnp.float32
BF16 = jnp.bfloat16

TALL = ROWS + 8
EARLY = (4, 3, 5, 2, 6)
LATE = (1, 7, 0)


def activate(values):
    return jax.nn.gelu(values, approximate=True)


def activate_slope(values):
    return jax.vjp(activate, values)[1](jnp.ones_like(values))[0]


def wanted_of(wanted_ref, y, delta, zo):
    owner = lax.rem(y + delta, NY) * NZ + zo
    return jnp.maximum(wanted_ref[2 * owner], wanted_ref[2 * owner + 1])


def pack_kernel(wanted_ref, place_ref, labels, *refs):
    outs, (held, in_sem, out_sem) = refs[:8], refs[8:]
    y = place_ref[0]
    z = place_ref[1]
    plan = []
    for wave, offsets in enumerate((EARLY, LATE)):
        for kind, delta in ((2, 2), (0, NY - 1), (1, 1)):
            for spot, offset in enumerate(offsets):
                plan.append((wave, kind, delta, spot, offset))
    ins = []
    for slot, (wave, kind, delta, spot, offset) in enumerate(plan):
        zo = lax.rem(z + offset, NZ)
        pick = jnp.maximum(wanted_of(wanted_ref, y, delta, zo), 0)
        copy = pltpu.make_async_copy(labels.at[pick], held.at[slot], in_sem.at[slot])
        copy.start()
        ins.append(copy)
    moves = []
    for slot, (wave, kind, delta, spot, offset) in enumerate(plan):
        ins[slot].wait()
        down, up, far_a, far_b = outs[4 * wave : 4 * wave + 4]
        if kind < 2:
            pairs = [(held.at[slot], (down, up)[kind].at[spot])]
        else:
            pairs = [
                (held.at[slot, :, pl.ds(0, HALF)], far_a.at[spot]),
                (held.at[slot, :, pl.ds(HALF, HALF)], far_b.at[spot]),
            ]
        for source, target in pairs:
            move = pltpu.make_async_copy(source, target, out_sem.at[len(moves)])
            move.start()
            moves.append(move)
    for move in moves:
        move.wait()


def pack(wanted, place, labels):
    any_spec = pl.BlockSpec(memory_space=pl.ANY)
    out_shape = []
    for offsets in (EARLY, LATE):
        for width in (D, D, HALF, HALF):
            out_shape.append(jax.ShapeDtypeStruct((len(offsets), BLK, width), BF16))
    return pl.pallas_call(
        pack_kernel,
        out_shape=tuple(out_shape),
        grid_spec=pltpu.PrefetchScalarGridSpec(
            num_scalar_prefetch=2,
            grid=(1,),
            in_specs=[any_spec],
            out_specs=[any_spec] * 8,
            scratch_shapes=[
                pltpu.VMEM((3 * NZ, BLK, D), BF16),
                pltpu.SemaphoreType.DMA((3 * NZ,)),
                pltpu.SemaphoreType.DMA((4 * NZ,)),
            ],
        ),
        cost_estimate=pl.CostEstimate(flops=0, bytes_accessed=10_000_000, transcendentals=0),
        name="pack",
    )(wanted, place, labels)


def meet_kernel(
    leading, carried,
    table_ref, wanted_ref, place_ref,
    rows_ref, own_ref, next_ref, far_a_ref, far_b_ref, prev_ref,
    *refs,
):
    refs = refs[carried:]
    part0_ref, part1_ref, part2a_ref, part2b_ref, part3_ref, grad_ref = refs[:6]
    labs = refs[-1]
    y = place_ref[0]
    zo = place_ref[2 + pl.program_id(0)]
    rows = rows_ref[:, :D]
    coded = rows_ref[:, D:].astype(F32)
    ids = [
        coded[:, 3 * n : 3 * n + 1] * 16384.0
        + coded[:, 3 * n + 1 : 3 * n + 2] * 128.0
        + coded[:, 3 * n + 2 : 3 * n + 3]
        for n in range(NPOS)
    ]
    labs[0:BLK, :] = own_ref[0]
    labs[BLK : 2 * BLK, :] = next_ref[0]
    labs[2 * BLK : 3 * BLK, :HALF] = far_a_ref[0]
    labs[2 * BLK : 3 * BLK, HALF:] = far_b_ref[0]
    labs[3 * BLK : 4 * BLK, :] = prev_ref[0]
    blocks_here = labs[...]
    logits = lax.dot_general(
        rows, blocks_here, (((1,), (1,)), ((), ())), preferred_element_type=F32
    )
    row_at = lax.broadcasted_iota(jnp.int32, (ROWS, BLK), 0)
    lane_at = lax.broadcasted_iota(jnp.int32, (ROWS, BLK), 1).astype(F32)
    loss = jnp.zeros((ROWS, BLK), F32)
    errors = []
    for delta in range(NY):
        holder_y = lax.rem(y + delta, NY)
        base = (y * NZ + zo) * 2 * NY + holder_y
        first = table_ref[base]
        second = table_ref[base + NY]
        block = (jnp.maximum(first, second) * BLK).astype(F32)
        live = jnp.where(row_at < CSIZE, first, second) >= 0
        here = logits[:, delta * BLK : (delta + 1) * BLK]
        hit = jnp.zeros((ROWS, BLK), jnp.bool_)
        for n in range(NPOS):
            hit = jnp.logical_or(hit, (ids[n] - block) == lane_at)
        targets = hit.astype(F32)
        tail = jnp.exp(-jnp.abs(here))
        soft = jnp.maximum(here, 0.0) + jnp.log1p(tail)
        part = 1.0 / (1.0 + tail)
        sig = jnp.where(here >= 0, part, tail * part)
        loss += jnp.where(live, soft - targets * here, 0.0)
        errors.append(jnp.where(live, sig - targets, 0.0).astype(BF16))
    errors = jnp.concatenate(errors, axis=1)
    grad = jnp.dot(errors, blocks_here, preferred_element_type=F32)
    parts = lax.dot_general(
        errors, rows, (((0,), (0,)), ((), ())), preferred_element_type=F32
    ).astype(BF16)
    part0_ref[0] = parts[0:BLK]
    part1_ref[0] = parts[BLK : 2 * BLK]
    part2a_ref[0] = parts[2 * BLK : 3 * BLK, :HALF]
    part2b_ref[0] = parts[2 * BLK : 3 * BLK, HALF:]
    part3_ref[0] = parts[3 * BLK : 4 * BLK]
    sums = lax.dot_general(
        jnp.ones((8, BLK), F32), loss, (((1,), (1,)), ((), ())),
        precision=lax.Precision.HIGHEST, preferred_element_type=F32,
    )
    extra = jnp.concatenate([sums, jnp.zeros((8, D - ROWS), F32)], axis=1)

    def keep():
        grad_ref[0, :ROWS] = grad
        grad_ref[0, ROWS:] = extra

    if leading:
        lead_ref, trail_ref = refs[6:8]

        @pl.when(pl.program_id(0) == 0)
        def _():
            lead_ref[...] = grad[:CSIZE].astype(BF16)
            trail_ref[:CSIZE] = grad[CSIZE:].astype(BF16)
            trail_ref[CSIZE:] = extra.astype(BF16)

        pl.when(pl.program_id(0) > 0)(keep)
    else:
        keep()


def meet(offsets, first, table, wanted, y, z, gathered, labels, blocks, parts=()):
    leading = not parts
    count = len(offsets)
    turns = offsets + offsets[-1:] * (6 - count)
    place = jnp.stack([y, z] + [(z + offset) % NZ for offset in turns]).astype(jnp.int32)

    def own_map(i, table_ref, wanted_ref, place_ref):
        pick = wanted_of(wanted_ref, place_ref[0], 0, place_ref[2 + i])
        return (jnp.maximum(pick, 0), 0, 0)

    def owner_map(i, table_ref, wanted_ref, place_ref):
        return (place_ref[2 + i], 0, 0)

    def grad_map(i, table_ref, wanted_ref, place_ref):
        return (jnp.maximum(i - 1, 0) if leading else i, 0, 0)

    def turn_map(i, table_ref, wanted_ref, place_ref):
        return (i + first, 0, 0)

    full = pl.BlockSpec((1, BLK, D), owner_map)
    half = pl.BlockSpec((1, BLK, HALF), owner_map)
    full_in = pl.BlockSpec((1, BLK, D), turn_map)
    half_in = pl.BlockSpec((1, BLK, HALF), turn_map)
    full_shape = jax.ShapeDtypeStruct((NZ, BLK, D), BF16)
    half_shape = jax.ShapeDtypeStruct((NZ, BLK, HALF), BF16)
    out_shape = [full_shape, full_shape, half_shape, half_shape, full_shape]
    out_shape.append(jax.ShapeDtypeStruct((count - leading, TALL, D), F32))
    out_specs = [full, full, half, half, full, pl.BlockSpec((1, TALL, D), grad_map)]
    if leading:
        for tall in (CSIZE, TALL - CSIZE):
            out_shape.append(jax.ShapeDtypeStruct((tall, D), BF16))
            out_specs.append(pl.BlockSpec((tall, D), lambda i, t, w, p: (0, 0)))
    return pl.pallas_call(
        functools.partial(meet_kernel, leading, len(parts)),
        out_shape=tuple(out_shape),
        grid_spec=pltpu.PrefetchScalarGridSpec(
            num_scalar_prefetch=3,
            grid=(count,),
            in_specs=[
                pl.BlockSpec((ROWS, D + ENC), lambda i, t, w, p: (p[2 + i], 0)),
                pl.BlockSpec((1, BLK, D), own_map),
                full_in, half_in, half_in, full_in,
            ] + [pl.BlockSpec(memory_space=pl.ANY)] * len(parts),
            out_specs=out_specs,
            scratch_shapes=[pltpu.VMEM((NY * BLK, D), BF16)],
        ),
        input_output_aliases={9 + n: n for n in range(len(parts))},
        cost_estimate=pl.CostEstimate(
            flops=600_000_000 * count, bytes_accessed=3_000_000 * count,
            transcendentals=400_000 * count,
        ),
        name="meet",
    )(table, wanted, place, gathered, labels, *blocks, *parts)


def fold_kernel(wanted_ref, place_ref, own, up, far_a, far_b, down, out, total):
    y = place_ref[0]
    total[...] = jnp.zeros_like(total)

    def one(zo, carry):
        for delta in range(NY):
            pick = wanted_of(wanted_ref, y, delta, zo)

            @pl.when(pick >= 0)
            def _():
                if delta == 2:
                    total[pick, :, :HALF] += far_a[zo].astype(F32)
                    total[pick, :, HALF:] += far_b[zo].astype(F32)
                else:
                    total[pick] += (own, up, None, down)[delta][zo].astype(F32)

        return carry

    lax.fori_loop(0, NZ, one, 0)

    def put(b, carry):
        out[b] = total[b].astype(BF16)
        return carry

    lax.fori_loop(0, BLK_DEV, put, 0)


def fold(wanted, place, own, up, far_a, far_b, down):
    vmem = pl.BlockSpec(memory_space=pltpu.VMEM)
    return pl.pallas_call(
        fold_kernel,
        out_shape=jax.ShapeDtypeStruct((BLK_DEV, BLK, D), BF16),
        grid_spec=pltpu.PrefetchScalarGridSpec(
            num_scalar_prefetch=2,
            grid=(1,),
            in_specs=[
                pl.BlockSpec((NZ, BLK, D), lambda i, w, p: (0, 0, 0)),
                pl.BlockSpec((NZ, BLK, D), lambda i, w, p: (0, 0, 0)),
                pl.BlockSpec((NZ, BLK, HALF), lambda i, w, p: (0, 0, 0)),
                pl.BlockSpec((NZ, BLK, HALF), lambda i, w, p: (0, 0, 0)),
                pl.BlockSpec((NZ, BLK, D), lambda i, w, p: (0, 0, 0)),
            ],
            out_specs=pl.BlockSpec((BLK_DEV, BLK, D), lambda i, w, p: (0, 0, 0)),
            scratch_shapes=[pltpu.VMEM((BLK_DEV, BLK, D), F32)],
        ),
        cost_estimate=pl.CostEstimate(flops=5_000_000, bytes_accessed=25_000_000, transcendentals=0),
        compiler_params=pltpu.CompilerParams(vmem_limit_bytes=48 * 1024 * 1024),
        name="fold",
    )(wanted, place, own, up, far_a, far_b, down)


def shift(values, axis, amount):
    size = lax.axis_size(axis)
    return lax.ppermute(values, axis, [(i, (i + amount) % size) for i in range(size)])


def scatter_sum(values, axis):
    size = lax.axis_size(axis)
    me = lax.axis_index(axis)
    step = values.shape[0] // size

    def piece(amount):
        at = lax.rem(me + amount, size) * step
        return lax.dynamic_slice_in_dim(values, at, step, 0)

    total = piece(0)
    for got in [shift(piece(amount), axis, amount) for amount in range(1, size)]:
        total = total + got
    return total


def gather_turns(values, axis):
    size = lax.axis_size(axis)
    return [values] + [shift(values, axis, amount) for amount in range(1, size)]


def spread_kernel(at_ref, *refs):
    sources, out = refs[:-1], refs[-1]
    x = at_ref[0]
    core = at_ref[1]
    y = at_ref[2]
    step = D // (2 * 4 * NY)
    for place, source in enumerate(sources):
        turn_x = place % 4
        side = core if place < 4 else 1 - core
        for turn_y in range(NY):
            to_x = lax.rem(x - turn_x + 4, 4)
            to_y = lax.rem(y - turn_y + NY, NY)
            to = pl.multiple_of(((side * 4 + to_x) * NY + to_y) * step, 8)
            out[pl.ds(to, step), :] = source[turn_y * step : (turn_y + 1) * step, :]


def spread(at, pieces):
    piece = pl.BlockSpec((D // 8, D), lambda i, a: (0, 0))
    return pl.pallas_call(
        spread_kernel,
        out_shape=jax.ShapeDtypeStruct((D, D), BF16),
        grid_spec=pltpu.PrefetchScalarGridSpec(
            num_scalar_prefetch=1,
            grid=(1,),
            in_specs=[piece] * len(pieces),
            out_specs=pl.BlockSpec((D, D), lambda i, a: (0, 0)),
        ),
        cost_estimate=pl.CostEstimate(flops=0, bytes_accessed=2_400_000, transcendentals=0),
        name="spread",
    )(at, *pieces)


def step(queries, query_slots, w_res, labels, blocks, positives):
    y = lax.axis_index("y")
    z = lax.axis_index("z")
    me = y * NZ + z
    group = lax.axis_index("x") * lax.axis_size("core") + lax.axis_index("core")
    devices = lax.axis_size("x") * lax.axis_size("core") * NDEV
    place = jnp.stack([y, z]).astype(jnp.int32)

    here = blocks - group * GRP_BLOCKS
    holder = here // BLK_DEV
    wanted = jnp.max(jnp.where(holder == me, here % BLK_DEV, -1), axis=1)
    columns = jnp.arange(NY, dtype=jnp.int32) * NZ + z
    table = jnp.max(
        jnp.where(holder[:, None, :] == columns[None, :, None], here[:, None, :], -1), axis=2
    ).reshape(-1)

    own_slots = lax.dynamic_slice_in_dim(query_slots, me * ROWS, ROWS)
    owner = own_slots // ROWS
    at = jnp.arange(ROWS, dtype=jnp.int32)
    rank = jnp.sum((owner[:, None] == owner[None, :]) & (at[:, None] < at[None, :]), axis=0)
    spot = owner * PER + rank
    sorter = (spot[None, :] == at[:, None]).astype(BF16)
    outbound = jnp.dot(sorter, queries, preferred_element_type=F32).astype(BF16)
    packed = pack(wanted, place, labels)
    arrived = lax.all_to_all(
        outbound.reshape(NDEV, PER, D), ("y", "z"), split_axis=0, concat_axis=0, tiled=True
    )
    arrived, _ = lax.optimization_barrier((arrived, packed[2]))
    arrived = arrived.reshape(ROWS, D)

    waves = []
    for down, up, far_a, far_b in (packed[:4], packed[4:]):
        far_a = shift(far_a, "y", 1)
        far_b = shift(far_b, "y", -1)
        prev = shift(up, "y", 1)
        nxt = shift(down, "y", -1)
        far_a = shift(far_a, "y", 1)
        far_b = shift(far_b, "y", -1)
        waves.append((nxt, far_a, far_b, prev))

    grid = query_slots.reshape(NDEV, ROWS)
    mine = grid // ROWS == me
    lower = (at[:, None] < at[None, :]).astype(BF16)
    before = jnp.dot(mine.astype(BF16), lower, preferred_element_type=F32).astype(jnp.int32)
    turn = jnp.arange(PER, dtype=jnp.int32)
    chosen = mine[:, None, :] & (before[:, None, :] == turn[None, :, None])
    incoming = jnp.sum(
        jnp.where(chosen, (grid - me * ROWS)[:, None, :], 0), axis=2
    ).reshape(ROWS)
    arrange = (incoming[None, :] == at[:, None]).astype(BF16)
    clustered_queries = jnp.dot(arrange, arrived, preferred_element_type=F32).astype(BF16)
    pre = jnp.dot(clustered_queries, w_res, preferred_element_type=F32)
    hidden = (clustered_queries.astype(F32) + activate(pre)).astype(BF16)

    label_at = positives - group * (GRP_BLOCKS * BLK)
    coded = jnp.stack([label_at // 16384, (label_at // 128) % 128, label_at % 128], axis=2)
    coded = jnp.pad(coded.reshape(ROWS, 3 * NPOS), ((0, 0), (0, ENC - 3 * NPOS))).astype(BF16)
    gathered = lax.all_gather(
        jnp.concatenate([hidden, coded], axis=1), "z", axis=0, tiled=True
    )

    common = (table, wanted, y, z, gathered, labels)
    *parts, grads_a, lead, trail = meet(EARLY[:3], 0, *common, waves[0])
    lead = shift(lead, "z", 1)
    trail = shift(trail, "z", -1)
    *parts, grads_b = meet(EARLY[3:], 3, *common, waves[0], parts=tuple(parts))
    lead = jnp.concatenate([lead.astype(F32) + grads_a[0, :CSIZE], grads_a[0, CSIZE:]])
    trail = jnp.concatenate([grads_a[1, :CSIZE], trail.astype(F32) + grads_a[1, CSIZE:]])
    lead = shift(lead.astype(BF16), "z", 1)
    trail = shift(trail.astype(BF16), "z", -1)
    *parts, grads_c = meet(LATE, 0, *common, waves[1], parts=tuple(parts))
    part0, part1, part2a, part2b, part3 = parts

    back2a = shift(part2a, "y", 1)
    back2b = shift(part2b, "y", -1)
    back1 = shift(part1, "y", 1)
    back3 = shift(part3, "y", -1)

    lead = shift((lead.astype(F32) + grads_b[0]).astype(BF16), "z", 1)
    trail = shift((trail.astype(F32) + grads_b[1]).astype(BF16), "z", -1)
    back2a = shift(back2a, "y", 1)
    back2b = shift(back2b, "y", -1)
    lead = shift((lead.astype(F32) + grads_c[0]).astype(BF16), "z", 1)
    trail = shift((trail.astype(F32) + grads_c[1]).astype(BF16), "z", -1)
    summed = lead.astype(F32) + trail.astype(F32) + grads_c[2]
    hidden_grad = summed[:ROWS].astype(BF16)
    query_loss = summed[ROWS, :ROWS] / float(SHORT * BLK)

    pre_grad = (hidden_grad.astype(F32) * activate_slope(pre)).astype(BF16)
    back = lax.dot_general(
        pre_grad, w_res, (((1,), (1,)), ((), ())), preferred_element_type=F32
    )
    query_rows = (hidden_grad.astype(F32) + back).astype(BF16)
    core = lax.axis_index("core")

    def term(side):
        columns = lax.dynamic_slice_in_dim(clustered_queries, side * HALF, HALF, 1)
        return lax.dot_general(
            columns, pre_grad, (((0,), (0,)), ((), ())), preferred_element_type=F32
        )

    other = shift(term(1 - core), "core", 1)
    total = term(core) + other
    total = scatter_sum(total, "x")
    total = scatter_sum(total, "y")
    whole = total
    for amount in range(1, NZ):
        whole = whole + shift(total, "z", amount)
    weight = (whole * float(ROWS * devices) ** (-0.5)).astype(BF16)
    weight = jnp.concatenate(gather_turns(weight, "y"), axis=0)
    pieces = gather_turns(weight, "x")
    pieces = pieces + [shift(piece, "core", 1) for piece in pieces]
    at_here = jnp.stack([lax.axis_index("x"), core, y]).astype(jnp.int32)
    weight = spread(at_here, pieces)

    returning = lax.dot_general(
        arrange, query_rows, (((0,), (0,)), ((), ())), preferred_element_type=F32
    ).astype(BF16)
    returned = lax.all_to_all(
        returning.reshape(NDEV, PER, D), ("y", "z"), split_axis=0, concat_axis=0, tiled=True
    ).reshape(ROWS, D)
    query_grad = lax.dot_general(
        sorter, returned, (((0,), (0,)), ((), ())), preferred_element_type=F32
    ).astype(BF16)

    label_grad = fold(wanted, place, part0, back3, back2a, back2b, back1)
    return query_loss, query_grad, label_grad, weight


def solution(mesh):
    inner = Mesh(
        mesh.devices.reshape(mesh.shape["grp"] // 2, 2, NY, NZ), ("x", "core", "y", "z")
    )
    every = ("x", "core", "y", "z")
    group = ("x", "core")
    in_specs = (
        P(every, None), P(group), P(), P(every, None, None), P(group, None), P(every, None),
    )
    out_specs = (P(every), P(every, None), P(every, None, None), P())
    return jax.shard_map(step, mesh=inner, in_specs=in_specs, out_specs=out_specs, check_vma=False)
```

```python
import functools

import jax
import jax.numpy as jnp
from jax import lax
from jax.experimental import pallas as pl
from jax.experimental.pallas import tpu as pltpu
from jax.sharding import Mesh, PartitionSpec as P


D = 768
HALF = D // 2
BLK = 128
CSIZE = 128
SHORT = 12
NPOS = 4
BLK_DEV = 20
CODES = 16
NY = 4
NZ = 8
NDEV = NY * NZ
ROWS = 2 * CSIZE
PER = ROWS // NDEV
GRP_BLOCKS = NDEV * BLK_DEV

F32 = jnp.float32
BF16 = jnp.bfloat16

TALL = ROWS + 8
EARLY = (4, 3, 5, 2, 6)
LATE = (1, 7, 0)


def activate(values):
    return jax.nn.gelu(values, approximate=True)


def activate_slope(values):
    return jax.vjp(activate, values)[1](jnp.ones_like(values))[0]


def wanted_of(wanted_ref, y, delta, zo):
    owner = lax.rem(y + delta, NY) * NZ + zo
    return jnp.maximum(wanted_ref[2 * owner], wanted_ref[2 * owner + 1])


def pack_kernel(wanted_ref, place_ref, labels, *refs):
    outs, (held, in_sem, out_sem) = refs[:8], refs[8:]
    y = place_ref[0]
    z = place_ref[1]
    plan = []
    for wave, offsets in enumerate((EARLY, LATE)):
        for kind, delta in ((2, 2), (0, NY - 1), (1, 1)):
            for spot, offset in enumerate(offsets):
                plan.append((wave, kind, delta, spot, offset))
    ins = []
    for slot, (wave, kind, delta, spot, offset) in enumerate(plan):
        zo = lax.rem(z + offset, NZ)
        pick = jnp.maximum(wanted_of(wanted_ref, y, delta, zo), 0)
        copy = pltpu.make_async_copy(labels.at[pick], held.at[slot], in_sem.at[slot])
        copy.start()
        ins.append(copy)
    moves = []
    for slot, (wave, kind, delta, spot, offset) in enumerate(plan):
        ins[slot].wait()
        down, up, far_a, far_b = outs[4 * wave : 4 * wave + 4]
        if kind < 2:
            pairs = [(held.at[slot], (down, up)[kind].at[spot])]
        else:
            pairs = [
                (held.at[slot, :, pl.ds(0, HALF)], far_a.at[spot]),
                (held.at[slot, :, pl.ds(HALF, HALF)], far_b.at[spot]),
            ]
        for source, target in pairs:
            move = pltpu.make_async_copy(source, target, out_sem.at[len(moves)])
            move.start()
            moves.append(move)
    for move in moves:
        move.wait()


def pack(wanted, place, labels):
    any_spec = pl.BlockSpec(memory_space=pl.ANY)
    out_shape = []
    for offsets in (EARLY, LATE):
        for width in (D, D, HALF, HALF):
            out_shape.append(jax.ShapeDtypeStruct((len(offsets), BLK, width), BF16))
    return pl.pallas_call(
        pack_kernel,
        out_shape=tuple(out_shape),
        grid_spec=pltpu.PrefetchScalarGridSpec(
            num_scalar_prefetch=2,
            grid=(1,),
            in_specs=[any_spec],
            out_specs=[any_spec] * 8,
            scratch_shapes=[
                pltpu.VMEM((3 * NZ, BLK, D), BF16),
                pltpu.SemaphoreType.DMA((3 * NZ,)),
                pltpu.SemaphoreType.DMA((4 * NZ,)),
            ],
        ),
        cost_estimate=pl.CostEstimate(flops=0, bytes_accessed=10_000_000, transcendentals=0),
        name="pack",
    )(wanted, place, labels)


def meet_kernel(
    leading, carried,
    table_ref, wanted_ref, place_ref,
    rows_ref, own_ref, next_ref, far_a_ref, far_b_ref, prev_ref,
    *refs,
):
    refs = refs[carried:]
    part0_ref, part1_ref, part2a_ref, part2b_ref, part3_ref, grad_ref = refs[:6]
    labs = refs[-1]
    y = place_ref[0]
    zo = place_ref[2 + pl.program_id(0)]
    rows = rows_ref[:ROWS, :]
    turn = lax.broadcasted_iota(jnp.int32, (CODES, BLK), 0)
    lane = lax.broadcasted_iota(jnp.int32, (CODES, BLK), 1)
    coded = lax.dot_general(
        rows_ref[ROWS:, :ROWS], (turn == lane).astype(F32).astype(BF16),
        (((0,), (0,)), ((), ())), preferred_element_type=F32,
    )
    ids = [
        coded[:, n : n + 1] * 16384.0
        + coded[:, NPOS + n : NPOS + n + 1] * 128.0
        + coded[:, 2 * NPOS + n : 2 * NPOS + n + 1]
        for n in range(NPOS)
    ]
    labs[0:BLK, :] = own_ref[0]
    labs[BLK : 2 * BLK, :] = next_ref[0]
    labs[2 * BLK : 3 * BLK, :HALF] = far_a_ref[0]
    labs[2 * BLK : 3 * BLK, HALF:] = far_b_ref[0]
    labs[3 * BLK : 4 * BLK, :] = prev_ref[0]
    blocks_here = labs[...]
    logits = lax.dot_general(
        rows, blocks_here, (((1,), (1,)), ((), ())), preferred_element_type=F32
    )
    row_at = lax.broadcasted_iota(jnp.int32, (ROWS, BLK), 0)
    lane_at = lax.broadcasted_iota(jnp.int32, (ROWS, BLK), 1).astype(F32)
    loss = jnp.zeros((ROWS, BLK), F32)
    errors = []
    for delta in range(NY):
        holder_y = lax.rem(y + delta, NY)
        base = (y * NZ + zo) * 2 * NY + holder_y
        first = table_ref[base]
        second = table_ref[base + NY]
        block = (jnp.maximum(first, second) * BLK).astype(F32)
        live = jnp.where(row_at < CSIZE, first, second) >= 0
        here = logits[:, delta * BLK : (delta + 1) * BLK]
        hit = jnp.zeros((ROWS, BLK), jnp.bool_)
        for n in range(NPOS):
            hit = jnp.logical_or(hit, (ids[n] - block) == lane_at)
        targets = hit.astype(F32)
        tail = jnp.exp(-jnp.abs(here))
        soft = jnp.maximum(here, 0.0) + jnp.log1p(tail)
        part = 1.0 / (1.0 + tail)
        sig = jnp.where(here >= 0, part, tail * part)
        loss += jnp.where(live, soft - targets * here, 0.0)
        errors.append(jnp.where(live, sig - targets, 0.0).astype(BF16))
    errors = jnp.concatenate(errors, axis=1)
    grad = jnp.dot(errors, blocks_here, preferred_element_type=F32)
    parts = lax.dot_general(
        errors, rows, (((0,), (0,)), ((), ())), preferred_element_type=F32
    ).astype(BF16)
    part0_ref[0] = parts[0:BLK]
    part1_ref[0] = parts[BLK : 2 * BLK]
    part2a_ref[0] = parts[2 * BLK : 3 * BLK, :HALF]
    part2b_ref[0] = parts[2 * BLK : 3 * BLK, HALF:]
    part3_ref[0] = parts[3 * BLK : 4 * BLK]
    sums = lax.dot_general(
        jnp.ones((8, BLK), F32), loss, (((1,), (1,)), ((), ())),
        precision=lax.Precision.HIGHEST, preferred_element_type=F32,
    )
    extra = jnp.concatenate([sums, jnp.zeros((8, D - ROWS), F32)], axis=1)

    def keep():
        grad_ref[0, :ROWS] = grad
        grad_ref[0, ROWS:] = extra

    if leading:
        lead_ref, trail_ref = refs[6:8]

        @pl.when(pl.program_id(0) == 0)
        def _():
            lead_ref[...] = grad[:CSIZE].astype(BF16)
            trail_ref[:CSIZE] = grad[CSIZE:].astype(BF16)
            trail_ref[CSIZE:] = extra.astype(BF16)

        pl.when(pl.program_id(0) > 0)(keep)
    else:
        keep()


def meet(offsets, first, table, wanted, y, z, gathered, labels, blocks, parts=()):
    leading = not parts
    count = len(offsets)
    turns = offsets + offsets[-1:] * (6 - count)
    place = jnp.stack([y, z] + [(z + offset) % NZ for offset in turns]).astype(jnp.int32)

    def own_map(i, table_ref, wanted_ref, place_ref):
        pick = wanted_of(wanted_ref, place_ref[0], 0, place_ref[2 + i])
        return (jnp.maximum(pick, 0), 0, 0)

    def owner_map(i, table_ref, wanted_ref, place_ref):
        return (place_ref[2 + i], 0, 0)

    def grad_map(i, table_ref, wanted_ref, place_ref):
        return (jnp.maximum(i - 1, 0) if leading else i, 0, 0)

    def turn_map(i, table_ref, wanted_ref, place_ref):
        return (i + first, 0, 0)

    full = pl.BlockSpec((1, BLK, D), owner_map)
    half = pl.BlockSpec((1, BLK, HALF), owner_map)
    full_in = pl.BlockSpec((1, BLK, D), turn_map)
    half_in = pl.BlockSpec((1, BLK, HALF), turn_map)
    full_shape = jax.ShapeDtypeStruct((NZ, BLK, D), BF16)
    half_shape = jax.ShapeDtypeStruct((NZ, BLK, HALF), BF16)
    out_shape = [full_shape, full_shape, half_shape, half_shape, full_shape]
    out_shape.append(jax.ShapeDtypeStruct((count - leading, TALL, D), F32))
    out_specs = [full, full, half, half, full, pl.BlockSpec((1, TALL, D), grad_map)]
    if leading:
        for tall in (CSIZE, TALL - CSIZE):
            out_shape.append(jax.ShapeDtypeStruct((tall, D), BF16))
            out_specs.append(pl.BlockSpec((tall, D), lambda i, t, w, p: (0, 0)))
    return pl.pallas_call(
        functools.partial(meet_kernel, leading, len(parts)),
        out_shape=tuple(out_shape),
        grid_spec=pltpu.PrefetchScalarGridSpec(
            num_scalar_prefetch=3,
            grid=(count,),
            in_specs=[
                pl.BlockSpec((ROWS + CODES, D), lambda i, t, w, p: (p[2 + i], 0)),
                pl.BlockSpec((1, BLK, D), own_map),
                full_in, half_in, half_in, full_in,
            ] + [pl.BlockSpec(memory_space=pl.ANY)] * len(parts),
            out_specs=out_specs,
            scratch_shapes=[pltpu.VMEM((NY * BLK, D), BF16)],
        ),
        input_output_aliases={9 + n: n for n in range(len(parts))},
        cost_estimate=pl.CostEstimate(
            flops=600_000_000 * count, bytes_accessed=3_000_000 * count,
            transcendentals=400_000 * count,
        ),
        name="meet",
    )(table, wanted, place, gathered, labels, *blocks, *parts)


def fold_kernel(wanted_ref, place_ref, own, up, far_a, far_b, down, out, total):
    y = place_ref[0]
    total[...] = jnp.zeros_like(total)

    def one(zo, carry):
        for delta in range(NY):
            pick = wanted_of(wanted_ref, y, delta, zo)

            @pl.when(pick >= 0)
            def _():
                if delta == 2:
                    total[pick, :, :HALF] += far_a[zo].astype(F32)
                    total[pick, :, HALF:] += far_b[zo].astype(F32)
                else:
                    total[pick] += (own, up, None, down)[delta][zo].astype(F32)

        return carry

    lax.fori_loop(0, NZ, one, 0)

    def put(b, carry):
        out[b] = total[b].astype(BF16)
        return carry

    lax.fori_loop(0, BLK_DEV, put, 0)


def fold(wanted, place, own, up, far_a, far_b, down):
    vmem = pl.BlockSpec(memory_space=pltpu.VMEM)
    return pl.pallas_call(
        fold_kernel,
        out_shape=jax.ShapeDtypeStruct((BLK_DEV, BLK, D), BF16),
        grid_spec=pltpu.PrefetchScalarGridSpec(
            num_scalar_prefetch=2,
            grid=(1,),
            in_specs=[
                pl.BlockSpec((NZ, BLK, D), lambda i, w, p: (0, 0, 0)),
                pl.BlockSpec((NZ, BLK, D), lambda i, w, p: (0, 0, 0)),
                pl.BlockSpec((NZ, BLK, HALF), lambda i, w, p: (0, 0, 0)),
                pl.BlockSpec((NZ, BLK, HALF), lambda i, w, p: (0, 0, 0)),
                pl.BlockSpec((NZ, BLK, D), lambda i, w, p: (0, 0, 0)),
            ],
            out_specs=pl.BlockSpec((BLK_DEV, BLK, D), lambda i, w, p: (0, 0, 0)),
            scratch_shapes=[pltpu.VMEM((BLK_DEV, BLK, D), F32)],
        ),
        cost_estimate=pl.CostEstimate(flops=5_000_000, bytes_accessed=25_000_000, transcendentals=0),
        compiler_params=pltpu.CompilerParams(vmem_limit_bytes=48 * 1024 * 1024),
        name="fold",
    )(wanted, place, own, up, far_a, far_b, down)


def shift(values, axis, amount):
    size = lax.axis_size(axis)
    return lax.ppermute(values, axis, [(i, (i + amount) % size) for i in range(size)])


def scatter_sum(values, axis):
    size = lax.axis_size(axis)
    me = lax.axis_index(axis)
    step = values.shape[0] // size

    def piece(amount):
        at = lax.rem(me + amount, size) * step
        return lax.dynamic_slice_in_dim(values, at, step, 0)

    total = piece(0)
    for got in [shift(piece(amount), axis, amount) for amount in range(1, size)]:
        total = total + got
    return total


def gather_turns(values, axis):
    size = lax.axis_size(axis)
    return [values] + [shift(values, axis, amount) for amount in range(1, size)]


def spread_kernel(at_ref, *refs):
    sources, out = refs[:-1], refs[-1]
    x = at_ref[0]
    core = at_ref[1]
    y = at_ref[2]
    step = D // (2 * 4 * NY)
    for place, source in enumerate(sources):
        turn_x = place % 4
        side = core if place < 4 else 1 - core
        for turn_y in range(NY):
            to_x = lax.rem(x - turn_x + 4, 4)
            to_y = lax.rem(y - turn_y + NY, NY)
            to = pl.multiple_of(((side * 4 + to_x) * NY + to_y) * step, 8)
            out[pl.ds(to, step), :] = source[turn_y * step : (turn_y + 1) * step, :]


def spread(at, pieces):
    piece = pl.BlockSpec((D // 8, D), lambda i, a: (0, 0))
    return pl.pallas_call(
        spread_kernel,
        out_shape=jax.ShapeDtypeStruct((D, D), BF16),
        grid_spec=pltpu.PrefetchScalarGridSpec(
            num_scalar_prefetch=1,
            grid=(1,),
            in_specs=[piece] * len(pieces),
            out_specs=pl.BlockSpec((D, D), lambda i, a: (0, 0)),
        ),
        cost_estimate=pl.CostEstimate(flops=0, bytes_accessed=2_400_000, transcendentals=0),
        name="spread",
    )(at, *pieces)


def step(queries, query_slots, w_res, labels, blocks, positives):
    y = lax.axis_index("y")
    z = lax.axis_index("z")
    me = y * NZ + z
    group = lax.axis_index("x") * lax.axis_size("core") + lax.axis_index("core")
    devices = lax.axis_size("x") * lax.axis_size("core") * NDEV
    place = jnp.stack([y, z]).astype(jnp.int32)

    here = blocks - group * GRP_BLOCKS
    holder = here // BLK_DEV
    wanted = jnp.max(jnp.where(holder == me, here % BLK_DEV, -1), axis=1)
    columns = jnp.arange(NY, dtype=jnp.int32) * NZ + z
    table = jnp.max(
        jnp.where(holder[:, None, :] == columns[None, :, None], here[:, None, :], -1), axis=2
    ).reshape(-1)

    own_slots = lax.dynamic_slice_in_dim(query_slots, me * ROWS, ROWS)
    owner = own_slots // ROWS
    at = jnp.arange(ROWS, dtype=jnp.int32)
    rank = jnp.sum((owner[:, None] == owner[None, :]) & (at[:, None] < at[None, :]), axis=0)
    spot = owner * PER + rank
    sorter = (spot[None, :] == at[:, None]).astype(BF16)
    outbound = jnp.dot(sorter, queries, preferred_element_type=F32).astype(BF16)
    packed = pack(wanted, place, labels)
    arrived = lax.all_to_all(
        outbound.reshape(NDEV, PER, D), ("y", "z"), split_axis=0, concat_axis=0, tiled=True
    )
    arrived, _ = lax.optimization_barrier((arrived, packed[2]))
    arrived = arrived.reshape(ROWS, D)

    waves = []
    for down, up, far_a, far_b in (packed[:4], packed[4:]):
        far_a = shift(far_a, "y", 1)
        far_b = shift(far_b, "y", -1)
        prev = shift(up, "y", 1)
        nxt = shift(down, "y", -1)
        far_a = shift(far_a, "y", 1)
        far_b = shift(far_b, "y", -1)
        waves.append((nxt, far_a, far_b, prev))

    grid = query_slots.reshape(NDEV, ROWS)
    mine = grid // ROWS == me
    lower = (at[:, None] < at[None, :]).astype(BF16)
    before = jnp.dot(mine.astype(BF16), lower, preferred_element_type=F32).astype(jnp.int32)
    turn = jnp.arange(PER, dtype=jnp.int32)
    chosen = mine[:, None, :] & (before[:, None, :] == turn[None, :, None])
    incoming = jnp.sum(
        jnp.where(chosen, (grid - me * ROWS)[:, None, :], 0), axis=2
    ).reshape(ROWS)
    arrange = (incoming[None, :] == at[:, None]).astype(BF16)
    clustered_queries = jnp.dot(arrange, arrived, preferred_element_type=F32).astype(BF16)
    pre = jnp.dot(clustered_queries, w_res, preferred_element_type=F32)
    hidden = (clustered_queries.astype(F32) + activate(pre)).astype(BF16)

    label_at = positives - group * (GRP_BLOCKS * BLK)
    label_at = label_at.T
    coded = jnp.concatenate([label_at // 16384, (label_at // 128) % 128, label_at % 128])
    coded = jnp.pad(coded, ((0, CODES - 3 * NPOS), (0, D - ROWS))).astype(BF16)
    gathered = lax.all_gather(jnp.concatenate([hidden, coded]), "z", axis=0, tiled=True)

    common = (table, wanted, y, z, gathered, labels)
    *parts, grads_a, lead, trail = meet(EARLY[:3], 0, *common, waves[0])
    lead = shift(lead, "z", 1)
    trail = shift(trail, "z", -1)
    *parts, grads_b = meet(EARLY[3:], 3, *common, waves[0], parts=tuple(parts))
    lead = jnp.concatenate([lead.astype(F32) + grads_a[0, :CSIZE], grads_a[0, CSIZE:]])
    trail = jnp.concatenate([grads_a[1, :CSIZE], trail.astype(F32) + grads_a[1, CSIZE:]])
    lead = shift(lead.astype(BF16), "z", 1)
    trail = shift(trail.astype(BF16), "z", -1)
    *parts, grads_c = meet(LATE, 0, *common, waves[1], parts=tuple(parts))
    part0, part1, part2a, part2b, part3 = parts

    back2a = shift(part2a, "y", 1)
    back2b = shift(part2b, "y", -1)
    back1 = shift(part1, "y", 1)
    back3 = shift(part3, "y", -1)

    lead = shift((lead.astype(F32) + grads_b[0]).astype(BF16), "z", 1)
    trail = shift((trail.astype(F32) + grads_b[1]).astype(BF16), "z", -1)
    back2a = shift(back2a, "y", 1)
    back2b = shift(back2b, "y", -1)
    lead = shift((lead.astype(F32) + grads_c[0]).astype(BF16), "z", 1)
    trail = shift((trail.astype(F32) + grads_c[1]).astype(BF16), "z", -1)
    summed = lead.astype(F32) + trail.astype(F32) + grads_c[2]
    hidden_grad = summed[:ROWS].astype(BF16)
    query_loss = summed[ROWS, :ROWS] / float(SHORT * BLK)

    pre_grad = (hidden_grad.astype(F32) * activate_slope(pre)).astype(BF16)
    back = lax.dot_general(
        pre_grad, w_res, (((1,), (1,)), ((), ())), preferred_element_type=F32
    )
    query_rows = (hidden_grad.astype(F32) + back).astype(BF16)
    core = lax.axis_index("core")

    def term(side):
        columns = lax.dynamic_slice_in_dim(clustered_queries, side * HALF, HALF, 1)
        return lax.dot_general(
            columns, pre_grad, (((0,), (0,)), ((), ())), preferred_element_type=F32
        )

    other = shift(term(1 - core), "core", 1)
    total = term(core) + other
    total = scatter_sum(total, "x")
    total = scatter_sum(total, "y")
    whole = total
    for amount in range(1, NZ):
        whole = whole + shift(total, "z", amount)
    weight = (whole * float(ROWS * devices) ** (-0.5)).astype(BF16)
    weight = jnp.concatenate(gather_turns(weight, "y"), axis=0)
    pieces = gather_turns(weight, "x")
    pieces = pieces + [shift(piece, "core", 1) for piece in pieces]
    at_here = jnp.stack([lax.axis_index("x"), core, y]).astype(jnp.int32)
    weight = spread(at_here, pieces)

    returning = lax.dot_general(
        arrange, query_rows, (((0,), (0,)), ((), ())), preferred_element_type=F32
    ).astype(BF16)
    returned = lax.all_to_all(
        returning.reshape(NDEV, PER, D), ("y", "z"), split_axis=0, concat_axis=0, tiled=True
    ).reshape(ROWS, D)
    query_grad = lax.dot_general(
        sorter, returned, (((0,), (0,)), ((), ())), preferred_element_type=F32
    ).astype(BF16)

    label_grad = fold(wanted, place, part0, back3, back2a, back2b, back1)
    return query_loss, query_grad, label_grad, weight


def solution(mesh):
    inner = Mesh(
        mesh.devices.reshape(mesh.shape["grp"] // 2, 2, NY, NZ), ("x", "core", "y", "z")
    )
    every = ("x", "core", "y", "z")
    group = ("x", "core")
    in_specs = (
        P(every, None), P(group), P(), P(every, None, None), P(group, None), P(every, None),
    )
    out_specs = (P(every), P(every, None), P(every, None, None), P())
    return jax.shard_map(step, mesh=inner, in_specs=in_specs, out_specs=out_specs, check_vma=False)
```

```python
import functools

import jax
import jax.numpy as jnp
from jax import lax
from jax.experimental import pallas as pl
from jax.experimental.pallas import tpu as pltpu
from jax.sharding import Mesh, PartitionSpec as P


D = 768
HALF = D // 2
BLK = 128
CSIZE = 128
SHORT = 12
NPOS = 4
BLK_DEV = 20
CODES = 16
NY = 4
NZ = 8
NDEV = NY * NZ
ROWS = 2 * CSIZE
PER = ROWS // NDEV
GRP_BLOCKS = NDEV * BLK_DEV

F32 = jnp.float32
BF16 = jnp.bfloat16

TALL = ROWS + 8
EARLY = (4, 3, 5, 2, 6)
LATE = (1, 7, 0)


def activate(values):
    return jax.nn.gelu(values, approximate=True)


def activate_slope(values):
    return jax.vjp(activate, values)[1](jnp.ones_like(values))[0]


def wanted_of(wanted_ref, y, delta, zo):
    owner = lax.rem(y + delta, NY) * NZ + zo
    return jnp.maximum(wanted_ref[2 * owner], wanted_ref[2 * owner + 1])


def pack_kernel(wanted_ref, place_ref, labels, *refs):
    outs, (held, in_sem, out_sem) = refs[:8], refs[8:]
    y = place_ref[0]
    z = place_ref[1]
    plan = []
    for wave, offsets in enumerate((EARLY, LATE)):
        for kind, delta in ((2, 2), (0, NY - 1), (1, 1)):
            for spot, offset in enumerate(offsets):
                plan.append((wave, kind, delta, spot, offset))
    ins = []
    for slot, (wave, kind, delta, spot, offset) in enumerate(plan):
        zo = lax.rem(z + offset, NZ)
        pick = jnp.maximum(wanted_of(wanted_ref, y, delta, zo), 0)
        copy = pltpu.make_async_copy(labels.at[pick], held.at[slot], in_sem.at[slot])
        copy.start()
        ins.append(copy)
    moves = []
    for slot, (wave, kind, delta, spot, offset) in enumerate(plan):
        ins[slot].wait()
        down, up, far_a, far_b = outs[4 * wave : 4 * wave + 4]
        if kind < 2:
            pairs = [(held.at[slot], (down, up)[kind].at[spot])]
        else:
            pairs = [
                (held.at[slot, :, pl.ds(0, HALF)], far_a.at[spot]),
                (held.at[slot, :, pl.ds(HALF, HALF)], far_b.at[spot]),
            ]
        for source, target in pairs:
            move = pltpu.make_async_copy(source, target, out_sem.at[len(moves)])
            move.start()
            moves.append(move)
    for move in moves:
        move.wait()


def pack(wanted, place, labels):
    any_spec = pl.BlockSpec(memory_space=pl.ANY)
    out_shape = []
    for offsets in (EARLY, LATE):
        for width in (D, D, HALF, HALF):
            out_shape.append(jax.ShapeDtypeStruct((len(offsets), BLK, width), BF16))
    return pl.pallas_call(
        pack_kernel,
        out_shape=tuple(out_shape),
        grid_spec=pltpu.PrefetchScalarGridSpec(
            num_scalar_prefetch=2,
            grid=(1,),
            in_specs=[any_spec],
            out_specs=[any_spec] * 8,
            scratch_shapes=[
                pltpu.VMEM((3 * NZ, BLK, D), BF16),
                pltpu.SemaphoreType.DMA((3 * NZ,)),
                pltpu.SemaphoreType.DMA((4 * NZ,)),
            ],
        ),
        cost_estimate=pl.CostEstimate(flops=0, bytes_accessed=10_000_000, transcendentals=0),
        name="pack",
    )(wanted, place, labels)


def meet_kernel(
    leading, carried,
    table_ref, wanted_ref, place_ref,
    rows_ref, own_ref, next_ref, far_a_ref, far_b_ref, prev_ref,
    *refs,
):
    refs = refs[carried:]
    part0_ref, part1_ref, part2a_ref, part2b_ref, part3_ref, grad_ref = refs[:6]
    labs = refs[-1]
    y = place_ref[0]
    zo = place_ref[2 + pl.program_id(0)]
    rows = rows_ref[:ROWS, :]
    turn = lax.broadcasted_iota(jnp.int32, (CODES, BLK), 0)
    lane = lax.broadcasted_iota(jnp.int32, (CODES, BLK), 1)
    coded = lax.dot_general(
        rows_ref[ROWS:, :ROWS], (turn == lane).astype(F32).astype(BF16),
        (((0,), (0,)), ((), ())), preferred_element_type=F32,
    )
    ids = [
        coded[:, n : n + 1] * 16384.0
        + coded[:, NPOS + n : NPOS + n + 1] * 128.0
        + coded[:, 2 * NPOS + n : 2 * NPOS + n + 1]
        for n in range(NPOS)
    ]
    labs[0:BLK, :] = own_ref[0]
    labs[BLK : 2 * BLK, :] = next_ref[0]
    labs[2 * BLK : 3 * BLK, :HALF] = far_a_ref[0]
    labs[2 * BLK : 3 * BLK, HALF:] = far_b_ref[0]
    labs[3 * BLK : 4 * BLK, :] = prev_ref[0]
    blocks_here = labs[...]
    logits = lax.dot_general(
        rows, blocks_here, (((1,), (1,)), ((), ())), preferred_element_type=F32
    )
    row_at = lax.broadcasted_iota(jnp.int32, (ROWS, BLK), 0)
    lane_at = lax.broadcasted_iota(jnp.int32, (ROWS, BLK), 1).astype(F32)
    loss = jnp.zeros((ROWS, BLK), F32)
    errors = []
    for delta in range(NY):
        holder_y = lax.rem(y + delta, NY)
        base = (y * NZ + zo) * 2 * NY + holder_y
        first = table_ref[base]
        second = table_ref[base + NY]
        block = (jnp.maximum(first, second) * BLK).astype(F32)
        live = jnp.where(row_at < CSIZE, first, second) >= 0
        here = logits[:, delta * BLK : (delta + 1) * BLK]
        hit = jnp.zeros((ROWS, BLK), jnp.bool_)
        for n in range(NPOS):
            hit = jnp.logical_or(hit, (ids[n] - block) == lane_at)
        targets = hit.astype(F32)
        tail = jnp.exp(-jnp.abs(here))
        soft = jnp.maximum(here, 0.0) + jnp.log1p(tail)
        part = 1.0 / (1.0 + tail)
        sig = jnp.where(here >= 0, part, tail * part)
        loss += jnp.where(live, soft - targets * here, 0.0)
        errors.append(jnp.where(live, sig - targets, 0.0).astype(BF16))
    errors = jnp.concatenate(errors, axis=1)
    grad = jnp.dot(errors, blocks_here, preferred_element_type=F32)
    parts = lax.dot_general(
        errors, rows, (((0,), (0,)), ((), ())), preferred_element_type=F32
    ).astype(BF16)
    part0_ref[0] = parts[0:BLK]
    part1_ref[0] = parts[BLK : 2 * BLK]
    part2a_ref[0] = parts[2 * BLK : 3 * BLK, :HALF]
    part2b_ref[0] = parts[2 * BLK : 3 * BLK, HALF:]
    part3_ref[0] = parts[3 * BLK : 4 * BLK]
    sums = lax.dot_general(
        jnp.ones((8, BLK), F32), loss, (((1,), (1,)), ((), ())),
        precision=lax.Precision.HIGHEST, preferred_element_type=F32,
    )
    extra = jnp.concatenate([sums, jnp.zeros((8, D - ROWS), F32)], axis=1)

    def keep():
        grad_ref[0, :ROWS] = grad
        grad_ref[0, ROWS:] = extra

    if leading:
        lead_ref, trail_ref = refs[6:8]

        @pl.when(pl.program_id(0) == 0)
        def _():
            lead_ref[...] = grad[:CSIZE].astype(BF16)
            trail_ref[:CSIZE] = grad[CSIZE:].astype(BF16)
            trail_ref[CSIZE:] = extra.astype(BF16)

        pl.when(pl.program_id(0) > 0)(keep)
    else:
        keep()


def meet(offsets, first, table, wanted, y, z, gathered, labels, blocks, parts=()):
    leading = not parts
    count = len(offsets)
    turns = offsets + offsets[-1:] * (6 - count)
    place = jnp.stack([y, z] + [(z + offset) % NZ for offset in turns]).astype(jnp.int32)

    def own_map(i, table_ref, wanted_ref, place_ref):
        pick = wanted_of(wanted_ref, place_ref[0], 0, place_ref[2 + i])
        return (jnp.maximum(pick, 0), 0, 0)

    def owner_map(i, table_ref, wanted_ref, place_ref):
        return (place_ref[2 + i], 0, 0)

    def grad_map(i, table_ref, wanted_ref, place_ref):
        return (jnp.maximum(i - 1, 0) if leading else i, 0, 0)

    def turn_map(i, table_ref, wanted_ref, place_ref):
        return (i + first, 0, 0)

    full = pl.BlockSpec((1, BLK, D), owner_map)
    half = pl.BlockSpec((1, BLK, HALF), owner_map)
    full_in = pl.BlockSpec((1, BLK, D), turn_map)
    half_in = pl.BlockSpec((1, BLK, HALF), turn_map)
    full_shape = jax.ShapeDtypeStruct((NZ, BLK, D), BF16)
    half_shape = jax.ShapeDtypeStruct((NZ, BLK, HALF), BF16)
    out_shape = [full_shape, full_shape, half_shape, half_shape, full_shape]
    out_shape.append(jax.ShapeDtypeStruct((count - leading, TALL, D), F32))
    out_specs = [full, full, half, half, full, pl.BlockSpec((1, TALL, D), grad_map)]
    if leading:
        for tall in (CSIZE, TALL - CSIZE):
            out_shape.append(jax.ShapeDtypeStruct((tall, D), BF16))
            out_specs.append(pl.BlockSpec((tall, D), lambda i, t, w, p: (0, 0)))
    return pl.pallas_call(
        functools.partial(meet_kernel, leading, len(parts)),
        out_shape=tuple(out_shape),
        grid_spec=pltpu.PrefetchScalarGridSpec(
            num_scalar_prefetch=3,
            grid=(count,),
            in_specs=[
                pl.BlockSpec((ROWS + CODES, D), lambda i, t, w, p: (p[2 + i], 0)),
                pl.BlockSpec((1, BLK, D), own_map),
                full_in, half_in, half_in, full_in,
            ] + [pl.BlockSpec(memory_space=pl.ANY)] * len(parts),
            out_specs=out_specs,
            scratch_shapes=[pltpu.VMEM((NY * BLK, D), BF16)],
        ),
        input_output_aliases={9 + n: n for n in range(len(parts))},
        cost_estimate=pl.CostEstimate(
            flops=600_000_000 * count, bytes_accessed=3_000_000 * count,
            transcendentals=400_000 * count,
        ),
        name="meet",
    )(table, wanted, place, gathered, labels, *blocks, *parts)


def fold_kernel(wanted_ref, place_ref, own, up, far_a, far_b, down, out, total):
    y = place_ref[0]
    total[...] = jnp.zeros_like(total)

    def one(zo, carry):
        for delta in range(NY):
            pick = wanted_of(wanted_ref, y, delta, zo)

            @pl.when(pick >= 0)
            def _():
                if delta == 2:
                    total[pick, :, :HALF] += far_a[zo].astype(F32)
                    total[pick, :, HALF:] += far_b[zo].astype(F32)
                else:
                    total[pick] += (own, up, None, down)[delta][zo].astype(F32)

        return carry

    lax.fori_loop(0, NZ, one, 0)

    def put(b, carry):
        out[b] = total[b].astype(BF16)
        return carry

    lax.fori_loop(0, BLK_DEV, put, 0)


def fold(wanted, place, own, up, far_a, far_b, down):
    vmem = pl.BlockSpec(memory_space=pltpu.VMEM)
    return pl.pallas_call(
        fold_kernel,
        out_shape=jax.ShapeDtypeStruct((BLK_DEV, BLK, D), BF16),
        grid_spec=pltpu.PrefetchScalarGridSpec(
            num_scalar_prefetch=2,
            grid=(1,),
            in_specs=[
                pl.BlockSpec((NZ, BLK, D), lambda i, w, p: (0, 0, 0)),
                pl.BlockSpec((NZ, BLK, D), lambda i, w, p: (0, 0, 0)),
                pl.BlockSpec((NZ, BLK, HALF), lambda i, w, p: (0, 0, 0)),
                pl.BlockSpec((NZ, BLK, HALF), lambda i, w, p: (0, 0, 0)),
                pl.BlockSpec((NZ, BLK, D), lambda i, w, p: (0, 0, 0)),
            ],
            out_specs=pl.BlockSpec((BLK_DEV, BLK, D), lambda i, w, p: (0, 0, 0)),
            scratch_shapes=[pltpu.VMEM((BLK_DEV, BLK, D), F32)],
        ),
        cost_estimate=pl.CostEstimate(flops=5_000_000, bytes_accessed=25_000_000, transcendentals=0),
        compiler_params=pltpu.CompilerParams(vmem_limit_bytes=48 * 1024 * 1024),
        name="fold",
    )(wanted, place, own, up, far_a, far_b, down)


def shift(values, axis, amount):
    size = lax.axis_size(axis)
    return lax.ppermute(values, axis, [(i, (i + amount) % size) for i in range(size)])


def scatter_sum(values, axis):
    size = lax.axis_size(axis)
    me = lax.axis_index(axis)
    step = values.shape[0] // size

    def piece(amount):
        at = lax.rem(me + amount, size) * step
        return lax.dynamic_slice_in_dim(values, at, step, 0)

    total = piece(0)
    for got in [shift(piece(amount), axis, amount) for amount in range(1, size)]:
        total = total + got
    return total


def gather_turns(values, axis):
    size = lax.axis_size(axis)
    return [values] + [shift(values, axis, amount) for amount in range(1, size)]


def spread_kernel(at_ref, *refs):
    sources, out = refs[:-1], refs[-1]
    x = at_ref[0]
    core = at_ref[1]
    y = at_ref[2]
    step = D // (2 * 4 * NY)
    for place, source in enumerate(sources):
        turn_x = place % 4
        side = core if place < 4 else 1 - core
        for turn_y in range(NY):
            to_x = lax.rem(x - turn_x + 4, 4)
            to_y = lax.rem(y - turn_y + NY, NY)
            to = pl.multiple_of(((side * 4 + to_x) * NY + to_y) * step, 8)
            out[pl.ds(to, step), :] = source[turn_y * step : (turn_y + 1) * step, :]


def spread(at, pieces):
    piece = pl.BlockSpec((D // 8, D), lambda i, a: (0, 0))
    return pl.pallas_call(
        spread_kernel,
        out_shape=jax.ShapeDtypeStruct((D, D), BF16),
        grid_spec=pltpu.PrefetchScalarGridSpec(
            num_scalar_prefetch=1,
            grid=(1,),
            in_specs=[piece] * len(pieces),
            out_specs=pl.BlockSpec((D, D), lambda i, a: (0, 0)),
        ),
        cost_estimate=pl.CostEstimate(flops=0, bytes_accessed=2_400_000, transcendentals=0),
        name="spread",
    )(at, *pieces)


def step(queries, query_slots, w_res, labels, blocks, positives):
    y = lax.axis_index("y")
    z = lax.axis_index("z")
    me = y * NZ + z
    group = lax.axis_index("x") * lax.axis_size("core") + lax.axis_index("core")
    devices = lax.axis_size("x") * lax.axis_size("core") * NDEV
    place = jnp.stack([y, z]).astype(jnp.int32)

    here = blocks - group * GRP_BLOCKS
    holder = here // BLK_DEV
    wanted = jnp.max(jnp.where(holder == me, here % BLK_DEV, -1), axis=1)
    columns = jnp.arange(NY, dtype=jnp.int32) * NZ + z
    table = jnp.max(
        jnp.where(holder[:, None, :] == columns[None, :, None], here[:, None, :], -1), axis=2
    ).reshape(-1)

    own_slots = lax.dynamic_slice_in_dim(query_slots, me * ROWS, ROWS)
    owner = own_slots // ROWS
    at = jnp.arange(ROWS, dtype=jnp.int32)
    rank = jnp.sum((owner[:, None] == owner[None, :]) & (at[:, None] < at[None, :]), axis=0)
    spot = owner * PER + rank
    sorter = (spot[None, :] == at[:, None]).astype(BF16)
    outbound = jnp.dot(sorter, queries, preferred_element_type=F32).astype(BF16)
    packed = pack(wanted, place, labels)
    arrived = lax.all_to_all(
        outbound.reshape(NDEV, PER, D), ("y", "z"), split_axis=0, concat_axis=0, tiled=True
    )
    arrived, _ = lax.optimization_barrier((arrived, packed[2]))
    arrived = arrived.reshape(ROWS, D)

    waves = []
    for down, up, far_a, far_b in (packed[:4], packed[4:]):
        far_a = shift(far_a, "y", 1)
        far_b = shift(far_b, "y", -1)
        prev = shift(up, "y", 1)
        nxt = shift(down, "y", -1)
        far_a = shift(far_a, "y", 1)
        far_b = shift(far_b, "y", -1)
        waves.append((nxt, far_a, far_b, prev))

    grid = query_slots.reshape(NDEV, ROWS)
    mine = grid // ROWS == me
    lower = (at[:, None] < at[None, :]).astype(BF16)
    before = jnp.dot(mine.astype(BF16), lower, preferred_element_type=F32).astype(jnp.int32)
    turn = jnp.arange(PER, dtype=jnp.int32)
    chosen = mine[:, None, :] & (before[:, None, :] == turn[None, :, None])
    incoming = jnp.sum(
        jnp.where(chosen, (grid - me * ROWS)[:, None, :], 0), axis=2
    ).reshape(ROWS)
    arrange = (incoming[None, :] == at[:, None]).astype(BF16)
    clustered_queries = jnp.dot(arrange, arrived, preferred_element_type=F32).astype(BF16)
    pre = jnp.dot(clustered_queries, w_res, preferred_element_type=F32)
    hidden = (clustered_queries.astype(F32) + activate(pre)).astype(BF16)

    label_at = positives - group * (GRP_BLOCKS * BLK)
    label_at = label_at.T
    coded = jnp.concatenate([label_at // 16384, (label_at // 128) % 128, label_at % 128])
    coded = jnp.pad(coded, ((0, CODES - 3 * NPOS), (0, D - ROWS))).astype(BF16)
    gathered = lax.all_gather(jnp.concatenate([hidden, coded]), "z", axis=0, tiled=True)

    common = (table, wanted, y, z, gathered, labels)
    *parts, grads_a, lead, trail = meet(EARLY[:3], 0, *common, waves[0])
    lead = shift(lead, "z", 1)
    trail = shift(trail, "z", -1)
    *parts, grads_b = meet(EARLY[3:], 3, *common, waves[0], parts=tuple(parts))
    lead = jnp.pad(lead.astype(F32), ((0, TALL - CSIZE), (0, 0))) + grads_a[0]
    trail = jnp.pad(trail.astype(F32), ((CSIZE, 0), (0, 0))) + grads_a[1]
    lead = shift(lead.astype(BF16), "z", 1)
    trail = shift(trail.astype(BF16), "z", -1)
    *parts, grads_c = meet(LATE, 0, *common, waves[1], parts=tuple(parts))
    part0, part1, part2a, part2b, part3 = parts

    back2a = shift(part2a, "y", 1)
    back2b = shift(part2b, "y", -1)
    back1 = shift(part1, "y", 1)
    back3 = shift(part3, "y", -1)

    lead = shift((lead.astype(F32) + grads_b[0]).astype(BF16), "z", 1)
    trail = shift((trail.astype(F32) + grads_b[1]).astype(BF16), "z", -1)
    back2a = shift(back2a, "y", 1)
    back2b = shift(back2b, "y", -1)
    lead = shift((lead.astype(F32) + grads_c[0]).astype(BF16), "z", 1)
    trail = shift((trail.astype(F32) + grads_c[1]).astype(BF16), "z", -1)
    summed = lead.astype(F32) + trail.astype(F32) + grads_c[2]
    hidden_grad = summed[:ROWS].astype(BF16)
    query_loss = summed[ROWS, :ROWS] / float(SHORT * BLK)

    pre_grad = (hidden_grad.astype(F32) * activate_slope(pre)).astype(BF16)
    back = lax.dot_general(
        pre_grad, w_res, (((1,), (1,)), ((), ())), preferred_element_type=F32
    )
    query_rows = (hidden_grad.astype(F32) + back).astype(BF16)
    core = lax.axis_index("core")

    def term(side):
        columns = lax.dynamic_slice_in_dim(clustered_queries, side * HALF, HALF, 1)
        return lax.dot_general(
            columns, pre_grad, (((0,), (0,)), ((), ())), preferred_element_type=F32
        )

    other = shift(term(1 - core), "core", 1)
    total = term(core) + other
    total = scatter_sum(total, "x")
    total = scatter_sum(total, "y")
    whole = total
    for bit in (1, 2, 4):
        whole = whole + lax.ppermute(whole, "z", [(i, i ^ bit) for i in range(NZ)])
    weight = (whole * float(ROWS * devices) ** (-0.5)).astype(BF16)
    weight = jnp.concatenate(gather_turns(weight, "y"), axis=0)
    pieces = gather_turns(weight, "x")
    pieces = pieces + [shift(piece, "core", 1) for piece in pieces]
    at_here = jnp.stack([lax.axis_index("x"), core, y]).astype(jnp.int32)
    weight = spread(at_here, pieces)

    returning = lax.dot_general(
        arrange, query_rows, (((0,), (0,)), ((), ())), preferred_element_type=F32
    ).astype(BF16)
    returned = lax.all_to_all(
        returning.reshape(NDEV, PER, D), ("y", "z"), split_axis=0, concat_axis=0, tiled=True
    ).reshape(ROWS, D)
    query_grad = lax.dot_general(
        sorter, returned, (((0,), (0,)), ((), ())), preferred_element_type=F32
    ).astype(BF16)

    label_grad = fold(wanted, place, part0, back3, back2a, back2b, back1)
    return query_loss, query_grad, label_grad, weight


def solution(mesh):
    inner = Mesh(
        mesh.devices.reshape(mesh.shape["grp"] // 2, 2, NY, NZ), ("x", "core", "y", "z")
    )
    every = ("x", "core", "y", "z")
    group = ("x", "core")
    in_specs = (
        P(every, None), P(group), P(), P(every, None, None), P(group, None), P(every, None),
    )
    out_specs = (P(every), P(every, None), P(every, None, None), P())
    return jax.shard_map(step, mesh=inner, in_specs=in_specs, out_specs=out_specs, check_vma=False)
```
